32 devices in a mesh: dp: 16 (over z, y, core), tensor: 2 (over x).
Axes of the slice: x: 2, y: 2, z: 4, core: 2. Of those that a mesh axis runs over, the one named last changes fastest.
Arguments:
- clip_feats: bfloat16 [2048, 1280], P('dp', 'tensor'), may hold values from -3 to 3
- proj_weight: bfloat16 [1280, 512], P('tensor'), may hold values from -1 to 1
- caption_emb: bfloat16 [2048, 512], P(('dp', 'tensor')), may hold values from -1.25 to 1.25
- logit_scale: float32 [1], replicated, may hold values from 20 to 400
- pair_perm: int32 [2048], replicated, may hold values from 0 to 2047, as said below
Outputs:
- clip_grad: float32 [2048, 1280], P('dp', 'tensor')
- caption_grad: float32 [2048, 512], P(('dp', 'tensor'))
- row_loss: float32 [2048], P('dp')
The draws below stay inside these ranges and needn't reach their ends.
Inputs may be any that keep to these rules, and one draw needn't show every extreme that they name: pair_perm is a permutation of the 2048 caption indices.
All inputs are finite; a program needn't handle non-finite values.
Results may differ from the reference program's by a relative error of at most 0.012.
The reference program's roundings to bfloat16 on the way (of `videos`, `captions`, `weights` and `raw_grad`) count: a program that leaves them out, or rounds other values in their place, can miss the bound.
Values may be sent and summed in bfloat16 or wider, within the bound.
A program may use at most 64 MiB of HBM per device.

```python
import math
import jax
import jax.numpy as jnp
from jax import lax

DV = 1280
E = 512
B = 2048


def shared_draw(key):
    pair_order = jax.random.permutation(jax.random.fold_in(key, 11), B).astype(jnp.int32)
    clip_base = jnp.clip(jax.random.normal(jax.random.fold_in(key, 12), (B, DV), jnp.float32), -6.0, 6.0) * 0.05
    proj_base = jnp.clip(jax.random.normal(jax.random.fold_in(key, 13), (DV, E), jnp.float32), -4.0, 4.0) / math.sqrt(DV)
    cap_base = jnp.clip(jax.random.normal(jax.random.fold_in(key, 14), (B, E), jnp.float32), -6.0, 6.0) * 0.05
    logit_value = jnp.exp(jax.random.uniform(jax.random.fold_in(key, 17), (1,), jnp.float32, math.log(20.0), math.log(100.0)))
    clip_feats = clip_base.astype(jnp.bfloat16)
    proj_weight = proj_base.astype(jnp.bfloat16)
    caption = cap_base
    return (clip_feats, proj_weight, caption.astype(jnp.bfloat16), logit_value, pair_order)


def draw_clip_feats(key, part):
    return shared_draw(key)[0]


def draw_proj_weight(key, part):
    return shared_draw(key)[1]


def draw_caption_emb(key, part):
    return shared_draw(key)[2]


def draw_logit_scale(key, part):
    return shared_draw(key)[3]


def draw_pair_perm(key, part):
    return shared_draw(key)[4]


def setup_inputs(seed: int = 0) -> dict:
    seeds = jax.random.split(jax.random.key(seed), 6)
    clip_feats = draw_clip_feats(jax.random.fold_in(seeds[5], 71), 0)
    proj_weight = draw_proj_weight(jax.random.fold_in(seeds[5], 71), 0)
    caption_emb = draw_caption_emb(jax.random.fold_in(seeds[5], 71), 0)
    logit_scale = draw_logit_scale(jax.random.fold_in(seeds[5], 71), 0)
    pair_perm = draw_pair_perm(jax.random.fold_in(seeds[5], 71), 0)
    return {"clip_feats": clip_feats, "proj_weight": proj_weight, "caption_emb": caption_emb, "logit_scale": logit_scale, "pair_perm": pair_perm}


norm_eps = 1e-06

def unit_rows(values):
    squares = lax.optimization_barrier(jnp.sum(values * values, axis=1, keepdims=True))
    inverse = lax.rsqrt(squares + norm_eps)
    return (values * inverse, inverse)

def reference(clip_feats, proj_weight, caption_emb, logit_scale, pair_perm):
    logit = logit_scale[0]
    raw_proj = jnp.dot(clip_feats, proj_weight, preferred_element_type=jnp.float32)
    unit_vid, vid_inv = unit_rows(raw_proj)
    videos = unit_vid.astype(jnp.bfloat16)
    cap_unit, cap_inv = unit_rows(caption_emb.astype(jnp.float32))
    captions = cap_unit.astype(jnp.bfloat16)
    row_count = videos.shape[0]
    width = captions.shape[1]
    row_block = math.gcd(row_count, 2048)
    block_count = row_count // row_block
    col_ids = jnp.arange(row_count, dtype=jnp.int32)

    def advance(cap_acc, block_index):
        offset = block_index * row_block
        vid_rows = lax.dynamic_slice_in_dim(videos, offset, row_block, 0)
        wanted = lax.dynamic_slice_in_dim(pair_perm, offset, row_block, 0)
        scores = logit * lax.dot_general(vid_rows, captions, (((1,), (1,)), ((), ())), preferred_element_type=jnp.float32)
        onehot = (col_ids[None, :] == wanted[:, None]).astype(jnp.float32)
        row_top = lax.optimization_barrier(jnp.max(scores, axis=1, keepdims=True))
        totals = lax.optimization_barrier(jnp.sum(jnp.exp(scores - row_top), axis=1, keepdims=True))
        positive = lax.optimization_barrier(jnp.sum(scores * onehot, axis=1))
        losses = row_top[:, 0] + jnp.log(totals[:, 0]) - positive
        weights = (jnp.exp(scores - row_top) / totals - onehot).astype(jnp.bfloat16)
        vid_grad = logit * jnp.dot(weights, captions, preferred_element_type=jnp.float32)
        cap_acc = cap_acc + logit * lax.dot_general(weights, vid_rows, (((0,), (0,)), ((), ())), preferred_element_type=jnp.float32)
        return (cap_acc, (losses, vid_grad))
    cap_grad, (losses, vid_grad) = lax.scan(advance, jnp.zeros((row_count, width), jnp.float32), jnp.arange(block_count, dtype=jnp.int32))
    losses = losses.reshape(row_count)
    vid_grad = vid_grad.reshape(row_count, width)
    vid_dot = lax.optimization_barrier(jnp.sum(unit_vid * vid_grad, axis=1, keepdims=True))
    raw_grad = ((vid_grad - unit_vid * vid_dot) * vid_inv).astype(jnp.bfloat16)
    clip_grad = lax.dot_general(raw_grad, proj_weight, (((1,), (1,)), ((), ())), preferred_element_type=jnp.float32)
    cap_dot = lax.optimization_barrier(jnp.sum(cap_unit * cap_grad, axis=1, keepdims=True))
    caption_grad = (cap_grad - cap_unit * cap_dot) * cap_inv
    return (clip_grad, caption_grad, losses)
```

```python
import functools

import jax
import jax.numpy as jnp
from jax import lax
from jax.experimental import pallas as pl
from jax.experimental.pallas import tpu as pltpu
from jax.sharding import PartitionSpec as P

norm_eps = 1e-06
MESH = pl.DeviceIdType.MESH
f32 = jnp.float32
bf16 = jnp.bfloat16


def split(dp):
    pair = 2 if dp % 2 == 0 else 1
    rest = dp // pair
    inner = max(n for n in range(1, rest + 1) if rest % n == 0 and n * n <= rest)
    return rest // inner, inner, pair


def chunks(rows):
    return max(n for n in (1, 2, 4) if rows % (16 * n) == 0 or n == 1)


def kernel(
    dp,
    tensor,
    logit_ref,
    perm_hbm,
    clip_hbm,
    proj_hbm,
    cap_hbm,
    clip_grad_ref,
    cap_grad_ref,
    loss_ref,
    perm_v,
    clip_v,
    proj_v,
    cap_v,
    part_own,
    part_send,
    part_recv,
    unit_vid,
    caps,
    vids,
    stats,
    loss_v,
    weights_v,
    cap_acc,
    row_part,
    row_send,
    row_recv,
    sum_send,
    sum_recv,
    pre_send,
    pre_recv,
    cap_send,
    cap_recv,
    load_sem,
    part_ss,
    part_rs,
    caps_ss,
    caps_rs,
    fwd_ss,
    fwd_rs,
    vids_ss,
    vids_rs,
    stats_ss,
    stats_rs,
    row_ss,
    row_rs,
    sum_ss,
    sum_rs,
    pre_ss,
    pre_rs,
    cg_ss,
    cg_rs,
):
    outer, inner, pair = split(dp)
    nb = inner * tensor
    rows, feats = clip_v.shape
    ccol, width = cap_v.shape
    tile_cols = outer * pair * ccol
    tile_rows = inner * rows
    nq = chunks(rows)
    pieces = [pl.ds(q * (rows // nq), rows // nq) for q in range(nq)]
    d = lax.axis_index("dp")
    t = lax.axis_index("tensor")
    c = lax.rem(d, pair)
    i = lax.rem(lax.div(d, pair), inner)
    z = lax.div(d, pair * inner)
    b = i * tensor + t

    def dp_index(zz, ii, cc):
        return (zz * inner + ii) * pair + cc

    def row_peer(k):
        pb = lax.rem(b + k, nb)
        return (dp_index(z, lax.div(pb, tensor), c), lax.rem(pb, tensor))

    def col_peer(k):
        pz = lax.rem(z + k, outer)
        return pz, (dp_index(pz, i, c), t)

    def inner_peer(k):
        pi = lax.rem(i + k, inner)
        return pi, (dp_index(z, pi, c), t)

    def core_peer():
        return (dp_index(z, i, pair - 1 - c), t)

    def tensor_peer(k):
        return (d, lax.rem(t + k, tensor))

    started = []

    def send(src, dst, ss, rs, device):
        copy = pltpu.make_async_remote_copy(
            src_ref=src, dst_ref=dst, send_sem=ss, recv_sem=rs, device_id=device, device_id_type=MESH
        )
        copy.start()
        started.append(copy)
        return copy

    loads = [
        pltpu.make_async_copy(src, dst, load_sem.at[n])
        for n, (src, dst) in enumerate(((cap_hbm, cap_v), (proj_hbm, proj_v), (clip_hbm, clip_v), (perm_hbm, perm_v)))
    ]
    for load in loads:
        load.start()
    barrier = pltpu.get_barrier_semaphore()
    peers = [row_peer(k) for k in range(1, nb)] + [col_peer(k)[1] for k in range(1, outer)]
    if pair > 1:
        peers.append(core_peer())
    for device in peers:
        pl.semaphore_signal(barrier, inc=1, device_id=device, device_id_type=MESH)

    loads[0].wait()
    cap_f = cap_v[...].astype(f32)
    cap_inv = lax.rsqrt(jnp.sum(cap_f * cap_f, axis=1, keepdims=True) + norm_eps)
    caps[c, z] = (cap_f * cap_inv).astype(bf16)
    pl.semaphore_wait(barrier, len(peers))
    far_first = sorted(range(1, outer), key=lambda k: -min(k, outer - k))
    cap_copies = {}
    for k in far_first:
        pz, dev = col_peer(k)
        cap_copies[k] = send(caps.at[c, z], caps.at[c, z], caps_ss.at[k - 1], caps_rs.at[k - 1], dev)
    fwd_copies = []
    if pair > 1:
        fwd_copies.append(send(caps.at[c, z], caps.at[c, z], fwd_ss.at[0], fwd_rs.at[0], core_peer()))
    loads[1].wait()
    loads[2].wait()
    part = jnp.dot(clip_v[...], proj_v[...], preferred_element_type=f32)
    part_own[...] = part
    part_send[...] = part.astype(bf16)
    part_copies = []
    for q, piece in enumerate(pieces):
        for k in range(1, tensor):
            src, dst = part_send.at[piece], part_recv.at[k - 1, piece]
            part_copies.append(send(src, dst, part_ss.at[k - 1, q], part_rs.at[k - 1, q], tensor_peer(k)))
    loads[3].wait()
    logit = logit_ref[0]

    vid_inv, vid_copies = [], []
    for q, piece in enumerate(pieces):
        raw_proj = part_own[piece]
        for k in range(1, tensor):
            part_copies[q * (tensor - 1) + k - 1].wait_recv()
            raw_proj = raw_proj + part_recv[k - 1, piece].astype(f32)
        inverse = lax.rsqrt(jnp.sum(raw_proj * raw_proj, axis=1, keepdims=True) + norm_eps)
        vid_inv.append(inverse)
        unit = raw_proj * inverse
        unit_vid[piece] = unit
        vids[i, piece] = unit.astype(bf16)
        for k in range(1, inner):
            here = vids.at[i, piece]
            vid_copies.append(send(here, here, vids_ss.at[k - 1, q], vids_rs.at[k - 1, q], inner_peer(k)[1]))
    for k in reversed(far_first):
        cap_copies[k].wait_recv()
        if pair > 1:
            pz = lax.rem(z + (outer - k), outer)
            fwd_copies.append(send(caps.at[c, pz], caps.at[c, pz], fwd_ss.at[k], fwd_rs.at[k], core_peer()))
    for copy in fwd_copies:
        copy.wait_recv()
    for copy in vid_copies:
        copy.wait_recv()

    captions = caps[...].reshape(tile_cols, width)
    videos = vids[...].reshape(tile_rows, width)
    scores = logit * lax.dot_general(captions, videos, (((1,), (1,)), ((), ())), preferred_element_type=f32)
    wanted = jnp.concatenate(
        [perm_v[:, pl.ds(pl.multiple_of(dp_index(z, n, c) * rows, rows), rows)] for n in range(inner)], axis=1
    )
    index = lax.broadcasted_iota(jnp.int32, (tile_cols, 1), 0)
    block = index // ccol
    column = (dp_index(block % outer, i, block // outer) * tensor + t) * ccol + index % ccol
    hit = column == wanted
    top = jnp.max(scores, axis=0, keepdims=True)
    expo = jnp.exp(scores - top)
    total = jnp.sum(expo, axis=0, keepdims=True)
    positive = jnp.sum(jnp.where(hit, scores, 0.0), axis=0, keepdims=True)
    stats[b] = jnp.concatenate([top, total, positive], axis=1)
    stat_copies = []
    for k in range(1, nb):
        stat_copies.append(send(stats.at[b], stats.at[b], stats_ss.at[k - 1], stats_rs.at[k - 1], row_peer(k)))
    for copy in stat_copies:
        copy.wait_recv()
    every = [stats[n] for n in range(nb)]
    tops = [v[:, :tile_rows] for v in every]
    row_max = functools.reduce(jnp.maximum, tops)
    row_sum = functools.reduce(
        jnp.add, [v[:, tile_rows : 2 * tile_rows] * jnp.exp(m - row_max) for v, m in zip(every, tops)]
    )
    row_pos = functools.reduce(jnp.add, [v[:, 2 * tile_rows :] for v in every])
    scale = jnp.exp(top - row_max) / row_sum
    weights = (expo * scale - hit.astype(f32)).astype(bf16)
    weights_v[...] = weights.reshape(pair, outer * ccol, tile_rows)

    near_last = [k for k in far_first] + [0]
    pre_copies = {}
    if pair > 1:
        part = jnp.dot(weights_v[pair - 1 - c], videos, preferred_element_type=f32)
        pre_send[...] = part.astype(bf16).reshape(outer, ccol, width)
        for k in near_last:
            pz = lax.rem(z + k, outer)
            pre_copies[k] = send(pre_send.at[pz], pre_recv.at[k], pre_ss.at[k], pre_rs.at[k], core_peer())
    vid_part = lax.dot_general(weights, captions, (((0,), (0,)), ((), ())), preferred_element_type=f32)
    row_part[...] = vid_part.reshape(inner, rows, width)
    row_send[...] = vid_part.astype(bf16).reshape(inner, rows, width)
    row_copies = []
    for q, piece in enumerate(pieces):
        for k in range(1, inner):
            pi, dev = inner_peer(k)
            src, dst = row_send.at[pi, piece], row_recv.at[k - 1, piece]
            row_copies.append(send(src, dst, row_ss.at[k - 1, q], row_rs.at[k - 1, q], dev))
    own = jnp.dot(weights_v[c], videos, preferred_element_type=f32)
    cap_acc[...] = own.reshape(outer, ccol, width)
    cg_copies = {}
    for k in near_last:
        pz, dev = col_peer(k)
        block_sum = cap_acc[pz]
        if pair > 1:
            pre_copies[k].wait_recv()
            block_sum = block_sum + pre_recv[k].astype(f32)
        if k > 0:
            cap_send[k - 1] = block_sum.astype(bf16)
            cg_copies[k] = send(cap_send.at[k - 1], cap_recv.at[k - 1], cg_ss.at[k - 1], cg_rs.at[k - 1], dev)
    cap_grad = block_sum
    sum_copies = []
    for q, piece in enumerate(pieces):
        row_sum_q = row_part[i, piece]
        for k in range(1, inner):
            row_copies[q * (inner - 1) + k - 1].wait_recv()
            row_sum_q = row_sum_q + row_recv[k - 1, piece].astype(f32)
        row_part[i, piece] = row_sum_q
        sum_send[piece] = row_sum_q.astype(bf16)
        for k in range(1, tensor):
            src, dst = sum_send.at[piece], sum_recv.at[k - 1, piece]
            sum_copies.append(send(src, dst, sum_ss.at[k - 1, q], sum_rs.at[k - 1, q], tensor_peer(k)))
    loss_v[...] = row_max + jnp.log(row_sum) - row_pos
    loss_ref[...] = loss_v[:, pl.ds(pl.multiple_of(i * rows, rows), rows)]
    for q, piece in enumerate(pieces):
        vid_grad = row_part[i, piece]
        for k in range(1, tensor):
            sum_copies[q * (tensor - 1) + k - 1].wait_recv()
            vid_grad = vid_grad + sum_recv[k - 1, piece].astype(f32)
        vid_grad = logit * vid_grad
        unit = unit_vid[piece]
        vid_dot = jnp.sum(unit * vid_grad, axis=1, keepdims=True)
        raw_grad = ((vid_grad - unit * vid_dot) * vid_inv[q]).astype(bf16)
        clip_grad_ref[piece] = lax.dot_general(
            raw_grad, proj_v[...], (((1,), (1,)), ((), ())), preferred_element_type=f32
        )
    for k in reversed(far_first):
        cg_copies[k].wait_recv()
        cap_grad = cap_grad + cap_recv[k - 1].astype(f32)
    cap_grad = logit * cap_grad
    cap_unit = cap_f * cap_inv
    cap_dot = jnp.sum(cap_unit * cap_grad, axis=1, keepdims=True)
    cap_grad_ref[...] = (cap_grad - cap_unit * cap_dot) * cap_inv
    for copy in started:
        copy.wait_send()


def store_kernel(*refs):
    count = len(refs) // 2
    sems = refs[-1]
    copies = [pltpu.make_async_copy(refs[n], refs[count + n], sems.at[n]) for n in range(count)]
    for copy in copies:
        copy.start()
    for copy in copies:
        copy.wait()


def store_results(*values):
    return pl.pallas_call(
        store_kernel,
        out_shape=tuple(jax.ShapeDtypeStruct(v.shape, v.dtype) for v in values),
        in_specs=[pl.BlockSpec(memory_space=pltpu.VMEM)] * len(values),
        out_specs=tuple(pl.BlockSpec(memory_space=pltpu.HBM) for v in values),
        scratch_shapes=[pltpu.SemaphoreType.DMA((len(values),))],
        compiler_params=pltpu.CompilerParams(vmem_limit_bytes=4 * 1024 * 1024),
        name="store_results",
    )(*values)


def body(dp, tensor, clip_feats, proj_weight, caption_emb, logit_scale, pair_perm):
    rows, feats = clip_feats.shape
    ccol, width = caption_emb.shape
    outer, inner, pair = split(dp)
    nb = inner * tensor
    tile_rows = inner * rows
    nq = chunks(rows)
    vmem = pl.BlockSpec(memory_space=pltpu.VMEM)
    hbm = pl.BlockSpec(memory_space=pltpu.HBM)
    dma = pltpu.SemaphoreType.DMA
    nr, no, nt, ni = max(nb - 1, 1), max(outer - 1, 1), max(tensor - 1, 1), max(inner - 1, 1)
    clip_grad, caption_grad, losses = pl.pallas_call(
        functools.partial(kernel, dp, tensor),
        out_shape=(
            jax.ShapeDtypeStruct((rows, feats), f32),
            jax.ShapeDtypeStruct((ccol, width), f32),
            jax.ShapeDtypeStruct((1, rows), f32),
        ),
        in_specs=[pl.BlockSpec(memory_space=pltpu.SMEM)] + [hbm] * 4,
        out_specs=(vmem, vmem, vmem),
        scratch_shapes=[
            pltpu.VMEM((1, pair_perm.shape[0]), jnp.int32),
            pltpu.VMEM((rows, feats), bf16),
            pltpu.VMEM(proj_weight.shape, bf16),
            pltpu.VMEM((ccol, width), bf16),
            pltpu.VMEM((rows, width), f32),
            pltpu.VMEM((rows, width), bf16),
            pltpu.VMEM((nt, rows, width), bf16),
            pltpu.VMEM((rows, width), f32),
            pltpu.VMEM((pair, outer, ccol, width), bf16),
            pltpu.VMEM((inner, rows, width), bf16),
            pltpu.VMEM((nb, 1, 3 * tile_rows), f32),
            pltpu.VMEM((1, tile_rows), f32),
            pltpu.VMEM((pair, outer * ccol, tile_rows), bf16),
            pltpu.VMEM((outer, ccol, width), f32),
            pltpu.VMEM((inner, rows, width), f32),
            pltpu.VMEM((inner, rows, width), bf16),
            pltpu.VMEM((ni, rows, width), bf16),
            pltpu.VMEM((rows, width), bf16),
            pltpu.VMEM((nt, rows, width), bf16),
            pltpu.VMEM((outer, ccol, width), bf16),
            pltpu.VMEM((outer, ccol, width), bf16),
            pltpu.VMEM((no, ccol, width), bf16),
            pltpu.VMEM((no, ccol, width), bf16),
            dma((4,)),
            *[dma((nt, nq))] * 2,
            *[dma((no,))] * 2,
            *[dma((outer,))] * 2,
            *[dma((ni, nq))] * 2,
            *[dma((nr,))] * 2,
            *[dma((ni, nq))] * 2,
            *[dma((nt, nq))] * 2,
            *[dma((outer,))] * 2,
            *[dma((no,))] * 2,
        ],
        compiler_params=pltpu.CompilerParams(collective_id=0, has_side_effects=True, vmem_limit_bytes=48 * 1024 * 1024),
        name="contrastive_step",
    )(
        logit_scale,
        *[
            pltpu.with_memory_space_constraint(x, pltpu.HBM)
            for x in (pair_perm.reshape(1, -1), clip_feats, proj_weight, caption_emb)
        ]
    )
    clip_grad, caption_grad, losses = store_results(clip_grad, caption_grad, losses)
    return clip_grad, caption_grad, losses.reshape(rows)


def solution(mesh):
    return jax.shard_map(
        functools.partial(body, mesh.shape["dp"], mesh.shape["tensor"]),
        mesh=mesh,
        in_specs=(P("dp", "tensor"), P("tensor", None), P(("dp", "tensor"), None), P(), P()),
        out_specs=(P("dp", "tensor"), P(("dp", "tensor"), None), P("dp")),
        check_vma=False,
    )
```

```python
import functools

import jax
import jax.numpy as jnp
from jax import lax
from jax.experimental import pallas as pl
from jax.experimental.pallas import tpu as pltpu
from jax.sharding import PartitionSpec as P

norm_eps = 1e-06
MESH = pl.DeviceIdType.MESH
f32 = jnp.float32
bf16 = jnp.bfloat16


def split(dp):
    pair = 2 if dp % 2 == 0 else 1
    rest = dp // pair
    inner = max(n for n in range(1, rest + 1) if rest % n == 0 and n * n <= rest)
    return rest // inner, inner, pair


def chunks(rows):
    return max(n for n in (1, 2, 4) if rows % (16 * n) == 0 or n == 1)


def direct(nq, nb):
    return nq // 2 if nb > 1 else 0


def depths(feats):
    size = 256 if feats > 256 else feats
    return [pl.ds(n, min(size, feats - n)) for n in range(0, feats, size)]


def inverse_norm(values):
    return lax.rsqrt(jnp.sum(values * values, axis=1, keepdims=True) + norm_eps)


def kernel(
    dp,
    tensor,
    logit_ref,
    perm_hbm,
    clip_hbm,
    proj_hbm,
    cap_hbm,
    clip_grad_ref,
    cap_grad_ref,
    loss_ref,
    perm_v,
    clip_v,
    proj_v,
    part_own,
    part_send,
    part_recv,
    part_dir,
    unit_vid,
    cap_v,
    caps,
    cap_unit,
    vids,
    stats,
    stats_recv,
    loss_v,
    weights_v,
    cap_acc,
    row_part,
    row_send,
    row_recv,
    sum_send,
    sum_recv,
    cap_send,
    cap_recv,
    load_sem,
    send_sem,
    part_rs,
    part_dir_rs,
    caps_rs,
    fwd_rs,
    vids_rs,
    stats_rs,
    row_rs,
    sum_rs,
    cross_rs,
    cg_rs,
):
    outer, inner, pair = split(dp)
    nb = inner * tensor
    rows, feats = clip_v.shape
    ccol, width = cap_hbm.shape
    tile_cols = outer * pair * ccol
    tile_rows = inner * rows
    nq = chunks(rows)
    step = rows // nq
    pieces = [pl.ds(q * step, step) for q in range(nq)]
    d = lax.axis_index("dp")
    t = lax.axis_index("tensor")
    c = lax.rem(d, pair)
    i = lax.rem(lax.div(d, pair), inner)
    z = lax.div(d, pair * inner)

    def dp_index(zz, ii, cc):
        return (zz * inner + ii) * pair + cc

    row_offsets = [(n, k) for n in range(inner) for k in range(tensor) if n or k]
    other_offsets = [(n, k) for n in range(inner) for k in range(tensor)] if pair > 1 else []

    def row_peer(n, k):
        pi = lax.rem(i + n, inner)
        return pi, (dp_index(z, pi, c), lax.rem(t + k, tensor))

    def other_peer(n, k):
        return (dp_index(z, lax.rem(i + n, inner), pair - 1 - c), lax.rem(t + k, tensor))

    def col_peer(k):
        pz = lax.rem(z + k, outer)
        return pz, (dp_index(pz, i, c), t)

    core_peer = (dp_index(z, i, pair - 1 - c), t)
    sent = {}

    def send(group, src, dst, rs, device):
        copy = pltpu.make_async_remote_copy(
            src_ref=src, dst_ref=dst, send_sem=send_sem.at[group], recv_sem=rs, device_id=device, device_id_type=MESH
        )
        copy.start()
        sent.setdefault(group, []).append(src)

    def wait(ref, sem):
        pltpu.make_async_copy(ref, ref, sem).wait()

    barrier = pltpu.get_barrier_semaphore()
    peers = [col_peer(k)[1] for k in range(1, outer)] + [row_peer(n, k)[1] for n, k in row_offsets]
    peers += [other_peer(n, k) for n, k in other_offsets]
    for device in peers:
        pl.semaphore_signal(barrier, inc=1, device_id=device, device_id_type=MESH)

    cuts = depths(feats)
    loads = [(cap_hbm, cap_v), (clip_hbm, clip_v)]
    loads += [(proj_hbm.at[cut], proj_v.at[cut]) for cut in cuts] + [(perm_hbm, perm_v)]
    loads = [pltpu.make_async_copy(src, dst, load_sem.at[n]) for n, (src, dst) in enumerate(loads)]
    for load in loads:
        load.start()
    loads[0].wait()
    raw_cap = cap_v[...].astype(f32)
    cap_inv = inverse_norm(raw_cap)
    unit_cap = raw_cap * cap_inv
    caps[c, z] = unit_cap.astype(bf16)
    loads[1].wait()
    part = None
    for n, cut in enumerate(cuts):
        loads[2 + n].wait()
        term = jnp.dot(clip_v[:, cut], proj_v[cut], preferred_element_type=f32)
        part = term if part is None else part + term
    part_own[...] = part
    part_send[...] = part.astype(bf16)
    pl.semaphore_wait(barrier, len(peers))
    own_caps = caps.at[c, z]
    far_first = sorted(range(1, outer), key=lambda k: -min(k, outer - k))
    for k in far_first:
        send(0, own_caps, own_caps, caps_rs.at[k - 1], col_peer(k)[1])
    if pair > 1:
        send(1, own_caps, own_caps, fwd_rs.at[0], core_peer)
    n1 = nq - direct(nq, nb)
    for q in range(n1):
        for k in range(1, tensor):
            send(2, part_send.at[pieces[q]], part_recv.at[k - 1, pieces[q]], part_rs.at[q], row_peer(0, k)[1])
    if n1 < nq:
        rest = pl.ds(n1 * step, rows - n1 * step)
        for n, k in row_offsets:
            place = n * tensor + k - 1
            send(3, part_send.at[rest], part_dir.at[place], part_dir_rs.at[0], row_peer(n, k)[1])
    cap_unit[...] = unit_cap
    loads[-1].wait()
    logit = logit_ref[0]

    vid_inv = [None] * nq
    for q in range(n1):
        piece = pieces[q]
        raw_proj = part_own[piece]
        if tensor > 1:
            wait(part_recv.at[:, piece], part_rs.at[q])
        for k in range(1, tensor):
            raw_proj = raw_proj + part_recv[k - 1, piece].astype(f32)
        vid_inv[q] = inverse_norm(raw_proj)
        unit = raw_proj * vid_inv[q]
        unit_vid[piece] = unit
        vids[c, i, piece] = unit.astype(bf16)
        for n in range(1, inner):
            here = vids.at[c, i, piece]
            send(4, here, here, vids_rs.at[n - 1, q], row_peer(n, 0)[1])
    for k in far_first[::-1][:-1]:
        pz = lax.rem(z + (outer - k), outer)
        wait(caps.at[c, pz], caps_rs.at[k - 1])
        if pair > 1:
            send(1, caps.at[c, pz], caps.at[c, pz], fwd_rs.at[k], core_peer)
    if n1 < nq:
        wait(part_dir, part_dir_rs.at[0])
        for n in range(inner):
            places = [n * tensor + k - 1 for k in range(tensor) if n or k]
            pi = lax.rem(i + (inner - n), inner)
            raw_proj = functools.reduce(
                jnp.add, ([] if n else [part_own[rest]]) + [part_dir[p].astype(f32) for p in places]
            )
            inverse = inverse_norm(raw_proj)
            unit = raw_proj * inverse
            vids[c, pi, rest] = unit.astype(bf16)
            if n == 0:
                unit_vid[rest] = unit
                for q in range(n1, nq):
                    vid_inv[q] = inverse[(q - n1) * step : (q - n1 + 1) * step]
    for k in far_first[:1]:
        pz = lax.rem(z + (outer - k), outer)
        wait(caps.at[c, pz], caps_rs.at[k - 1])
        if pair > 1:
            send(1, caps.at[c, pz], caps.at[c, pz], fwd_rs.at[k], core_peer)
    for n in range(1, inner):
        pi = lax.rem(i + (inner - n), inner)
        for q in range(n1):
            wait(vids.at[c, pi, pieces[q]], vids_rs.at[n - 1, q])

    if pair > 1:
        send(6, vids.at[c], vids.at[c], cross_rs.at[0], core_peer)
    half = outer * ccol
    index = lax.broadcasted_iota(jnp.int32, (half, 1), 0)

    def score(cc, rc):
        columns = caps[cc].reshape(half, width)
        videos = vids[rc].reshape(tile_rows, width)
        values = logit * lax.dot_general(columns, videos, (((1,), (1,)), ((), ())), preferred_element_type=f32)
        wanted = jnp.concatenate(
            [perm_v[:, pl.ds(pl.multiple_of(dp_index(z, n, rc) * rows, rows), rows)] for n in range(inner)], axis=1
        )
        return values, (dp_index(index // ccol, i, cc) * tensor + t) * ccol + index % ccol == wanted

    tiles = [score(c, c)]
    if pair > 1:
        for k in range(outer):
            pz = lax.rem(z + (outer - k), outer)
            wait(caps.at[1 - c, pz], fwd_rs.at[k])
        tiles.append(score(1 - c, c))
    top = functools.reduce(jnp.maximum, [jnp.max(v, axis=0, keepdims=True) for v, _ in tiles])
    expo = [jnp.exp(tile[0] - top) for tile in tiles]
    total = functools.reduce(jnp.add, [jnp.sum(v, axis=0, keepdims=True) for v in expo])
    positive = functools.reduce(jnp.add, [jnp.sum(jnp.where(h, v, 0.0), axis=0, keepdims=True) for v, h in tiles])
    stats[...] = jnp.concatenate([top, total, positive], axis=1)
    for n, k in row_offsets:
        send(5, stats, stats_recv.at[n * tensor + k - 1], stats_rs.at[0], row_peer(n, k)[1])
    for n, k in other_offsets:
        send(5, stats, stats_recv.at[nb - 1 + n * tensor + k], stats_rs.at[0], other_peer(n, k))
    if pair > 1:
        wait(vids.at[1 - c], cross_rs.at[0])
        cross, cross_hit = score(c, 1 - c)
    if pair * nb > 1:
        wait(stats_recv, stats_rs.at[0])

    def combine(every):
        tops = [v[:, :tile_rows] for v in every]
        row_max = functools.reduce(jnp.maximum, tops)
        sums = [v[:, tile_rows : 2 * tile_rows] * jnp.exp(m - row_max) for v, m in zip(every, tops)]
        return row_max, functools.reduce(jnp.add, sums)

    every = [stats[...]] + [stats_recv[n] for n in range(nb - 1)]
    row_max, row_sum = combine(every)
    row_pos = functools.reduce(jnp.add, [v[:, 2 * tile_rows :] for v in every])
    scale = jnp.exp(top - row_max) / row_sum
    weights = [(v * scale - tile[1].astype(f32)).astype(bf16) for v, tile in zip(expo, tiles)]

    def vid_rows(pi):
        cols = pl.ds(pl.multiple_of(pi * rows, rows), rows)
        terms = [
            lax.dot_general(
                weights_v[n, :, cols], caps[cc].reshape(half, width), (((0,), (0,)), ((), ())), preferred_element_type=f32
            )
            for n, cc in enumerate((c, 1 - c)[:pair])
        ]
        return functools.reduce(jnp.add, terms)

    for n, v in enumerate(weights):
        weights_v[n] = v
    for n in range(1, inner):
        pi, dev = row_peer(n, 0)
        row_send[n - 1] = vid_rows(pi).astype(bf16)
        for q in range(nq):
            send(7, row_send.at[n - 1, pieces[q]], row_recv.at[n - 1, pieces[q]], row_rs.at[n - 1, q], dev)
    own = jnp.dot(weights[0], vids[c].reshape(tile_rows, width), preferred_element_type=f32)
    if pair > 1:
        cross_max, cross_sum = combine([stats_recv[nb - 1 + n] for n in range(nb)])
        cross = (jnp.exp(cross - cross_max) / cross_sum - cross_hit.astype(f32)).astype(bf16)
        own = own + jnp.dot(cross, vids[1 - c].reshape(tile_rows, width), preferred_element_type=f32)
    cap_acc[...] = own.reshape(outer, ccol, width)
    for k in far_first:
        pz, dev = col_peer(k)
        cap_send[k - 1] = cap_acc[pz].astype(bf16)
        send(9, cap_send.at[k - 1], cap_recv.at[k - 1], cg_rs.at[k - 1], dev)
    row_part[...] = vid_rows(i)
    loss_v[...] = row_max + jnp.log(row_sum) - row_pos
    loss_ref[...] = loss_v[:, pl.ds(pl.multiple_of(i * rows, rows), rows)]

    def clip_rows(piece, vid_grad, inverse):
        vid_grad = logit * vid_grad
        unit = unit_vid[piece]
        vid_dot = jnp.sum(unit * vid_grad, axis=1, keepdims=True)
        raw_grad = ((vid_grad - unit * vid_dot) * inverse).astype(bf16)
        clip_grad_ref[piece] = lax.dot_general(
            raw_grad, proj_v[...], (((1,), (1,)), ((), ())), preferred_element_type=f32
        )

    for q in range(nq):
        piece = pieces[q]
        piece_sum = row_part[piece]
        for n in range(1, inner):
            wait(row_recv.at[n - 1, piece], row_rs.at[n - 1, q])
            piece_sum = piece_sum + row_recv[n - 1, piece].astype(f32)
        row_part[piece] = piece_sum
        sum_send[piece] = piece_sum.astype(bf16)
        for k in range(1, tensor):
            send(10, sum_send.at[piece], sum_recv.at[k - 1, piece], sum_rs.at[q], row_peer(0, k)[1])
    for q in range(nq):
        piece = pieces[q]
        vid_grad = row_part[piece]
        if tensor > 1:
            wait(sum_recv.at[:, piece], sum_rs.at[q])
        for k in range(1, tensor):
            vid_grad = vid_grad + sum_recv[k - 1, piece].astype(f32)
        clip_rows(piece, vid_grad, vid_inv[q])
    cap_grad = cap_acc[z]
    for k in reversed(far_first):
        wait(cap_recv.at[k - 1], cg_rs.at[k - 1])
        cap_grad = cap_grad + cap_recv[k - 1].astype(f32)
    cap_grad = logit * cap_grad
    unit = cap_unit[...]
    cap_dot = jnp.sum(unit * cap_grad, axis=1, keepdims=True)
    cap_grad_ref[...] = (cap_grad - unit * cap_dot) * cap_inv
    for group, refs in sent.items():
        for ref in refs:
            wait(ref, send_sem.at[group])


def store_kernel(*refs):
    count = len(refs) // 2
    sems = refs[-1]
    copies = [pltpu.make_async_copy(refs[n], refs[count + n], sems.at[n]) for n in range(count)]
    for copy in copies:
        copy.start()
    for copy in copies:
        copy.wait()


def store_results(*values):
    return pl.pallas_call(
        store_kernel,
        out_shape=tuple(jax.ShapeDtypeStruct(v.shape, v.dtype) for v in values),
        in_specs=[pl.BlockSpec(memory_space=pltpu.VMEM)] * len(values),
        out_specs=tuple(pl.BlockSpec(memory_space=pltpu.HBM) for v in values),
        scratch_shapes=[pltpu.SemaphoreType.DMA((len(values),))],
        compiler_params=pltpu.CompilerParams(vmem_limit_bytes=4 * 1024 * 1024),
        name="store_results",
    )(*values)


def body(dp, tensor, clip_feats, proj_weight, caption_emb, logit_scale, pair_perm):
    rows, feats = clip_feats.shape
    ccol, width = caption_emb.shape
    outer, inner, pair = split(dp)
    nb = inner * tensor
    tile_rows = inner * rows
    nq = chunks(rows)
    vmem = pl.BlockSpec(memory_space=pltpu.VMEM)
    hbm = pl.BlockSpec(memory_space=pltpu.HBM)
    dma = pltpu.SemaphoreType.DMA
    nr, no, nt, ni = max(nb - 1, 1), max(outer - 1, 1), max(tensor - 1, 1), max(inner - 1, 1)
    nd1 = direct(nq, nb)
    clip_grad, caption_grad, losses = pl.pallas_call(
        functools.partial(kernel, dp, tensor),
        out_shape=(
            jax.ShapeDtypeStruct((rows, feats), f32),
            jax.ShapeDtypeStruct((ccol, width), f32),
            jax.ShapeDtypeStruct((1, rows), f32),
        ),
        in_specs=[pl.BlockSpec(memory_space=pltpu.SMEM)] + [hbm] * 4,
        out_specs=(vmem, vmem, vmem),
        scratch_shapes=[
            pltpu.VMEM((1, pair_perm.shape[0]), jnp.int32),
            pltpu.VMEM((rows, feats), bf16),
            pltpu.VMEM(proj_weight.shape, bf16),
            pltpu.VMEM((rows, width), f32),
            pltpu.VMEM((rows, width), bf16),
            pltpu.VMEM((nt, rows, width), bf16),
            pltpu.VMEM((nr, max(nd1, 1) * (rows // nq), width), bf16),
            pltpu.VMEM((rows, width), f32),
            pltpu.VMEM((ccol, width), bf16),
            pltpu.VMEM((pair, outer, ccol, width), bf16),
            pltpu.VMEM((ccol, width), f32),
            pltpu.VMEM((pair, inner, rows, width), bf16),
            pltpu.VMEM((1, 3 * tile_rows), f32),
            pltpu.VMEM((max(pair * nb - 1, 1), 1, 3 * tile_rows), f32),
            pltpu.VMEM((1, tile_rows), f32),
            pltpu.VMEM((pair, outer * ccol, tile_rows), bf16),
            pltpu.VMEM((outer, ccol, width), f32),
            pltpu.VMEM((rows, width), f32),
            pltpu.VMEM((ni, rows, width), bf16),
            pltpu.VMEM((ni, rows, width), bf16),
            pltpu.VMEM((rows, width), bf16),
            pltpu.VMEM((nt, rows, width), bf16),
            pltpu.VMEM((no, ccol, width), bf16),
            pltpu.VMEM((no, ccol, width), bf16),
            dma((len(depths(feats)) + 3,)),
            dma((11,)),
            dma((max(nq - nd1, 1),)),
            dma((1,)),
            dma((no,)),
            dma((outer,)),
            dma((ni, max(nq - nd1, 1))),
            dma((1,)),
            dma((ni, nq)),
            dma((nq,)),
            dma((1,)),
            dma((no,)),
        ],
        compiler_params=pltpu.CompilerParams(collective_id=0, has_side_effects=True, vmem_limit_bytes=48 * 1024 * 1024),
        name="contrastive_step",
    )(
        logit_scale,
        *[
            pltpu.with_memory_space_constraint(x, pltpu.HBM)
            for x in (pair_perm.reshape(1, -1), clip_feats, proj_weight, caption_emb)
        ]
    )
    clip_grad, caption_grad, losses = store_results(clip_grad, caption_grad, losses)
    return clip_grad, caption_grad, losses.reshape(rows)


def solution(mesh):
    return jax.shard_map(
        functools.partial(body, mesh.shape["dp"], mesh.shape["tensor"]),
        mesh=mesh,
        in_specs=(P("dp", "tensor"), P("tensor", None), P(("dp", "tensor"), None), P(), P()),
        out_specs=(P("dp", "tensor"), P(("dp", "tensor"), None), P("dp")),
        check_vma=False,
    )
```

```python
import functools

import jax
import jax.numpy as jnp
from jax import lax
from jax.experimental import pallas as pl
from jax.experimental.pallas import tpu as pltpu
from jax.sharding import PartitionSpec as P

norm_eps = 1e-06
MESH = pl.DeviceIdType.MESH
f32 = jnp.float32
bf16 = jnp.bfloat16


def split(dp):
    pair = 2 if dp % 2 == 0 else 1
    rest = dp // pair
    inner = max(n for n in range(1, rest + 1) if rest % n == 0 and n * n <= rest)
    return rest // inner, inner, pair


def chunks(rows):
    return max(n for n in (1, 2, 4) if rows % (16 * n) == 0 or n == 1)


def direct(nq, nb):
    return nq // 2 if nb > 1 else 0


def direct_back(nq, nb):
    return 2 * nq // 4 if nb > 1 else 0


def depths(feats):
    size = 256 if feats > 256 else feats
    return [pl.ds(n, min(size, feats - n)) for n in range(0, feats, size)]


def inverse_norm(values):
    return lax.rsqrt(jnp.sum(values * values, axis=1, keepdims=True) + norm_eps)


def kernel(
    dp,
    tensor,
    logit_ref,
    perm_hbm,
    clip_hbm,
    proj_hbm,
    cap_hbm,
    clip_grad_ref,
    cap_grad_ref,
    loss_ref,
    perm_v,
    clip_v,
    proj_v,
    part_own,
    part_send,
    part_recv,
    part_dir,
    unit_vid,
    cap_v,
    caps,
    cap_unit,
    vids,
    stats,
    stats_recv,
    loss_v,
    weights_v,
    cap_acc,
    row_part,
    row_send,
    row_recv,
    row_dir,
    sum_send,
    sum_recv,
    cap_send,
    cap_recv,
    load_sem,
    send_sem,
    part_rs,
    part_dir_rs,
    caps_rs,
    fwd_rs,
    vids_rs,
    stats_rs,
    row_rs,
    row_dir_rs,
    sum_rs,
    cross_rs,
    cg_rs,
):
    outer, inner, pair = split(dp)
    nb = inner * tensor
    rows, feats = clip_v.shape
    ccol, width = cap_hbm.shape
    tile_cols = outer * pair * ccol
    tile_rows = inner * rows
    nq = chunks(rows)
    step = rows // nq
    pieces = [pl.ds(q * step, step) for q in range(nq)]
    d = lax.axis_index("dp")
    t = lax.axis_index("tensor")
    c = lax.rem(d, pair)
    i = lax.rem(lax.div(d, pair), inner)
    z = lax.div(d, pair * inner)

    def dp_index(zz, ii, cc):
        return (zz * inner + ii) * pair + cc

    row_offsets = [(n, k) for n in range(inner) for k in range(tensor) if n or k]
    other_offsets = [(n, k) for n in range(inner) for k in range(tensor)] if pair > 1 else []

    def row_peer(n, k):
        pi = lax.rem(i + n, inner)
        return pi, (dp_index(z, pi, c), lax.rem(t + k, tensor))

    def other_peer(n, k):
        return (dp_index(z, lax.rem(i + n, inner), pair - 1 - c), lax.rem(t + k, tensor))

    def col_peer(k):
        pz = lax.rem(z + k, outer)
        return pz, (dp_index(pz, i, c), t)

    core_peer = (dp_index(z, i, pair - 1 - c), t)
    sent = {}

    def send(group, src, dst, rs, device):
        copy = pltpu.make_async_remote_copy(
            src_ref=src, dst_ref=dst, send_sem=send_sem.at[group], recv_sem=rs, device_id=device, device_id_type=MESH
        )
        copy.start()
        sent.setdefault(group, []).append(src)

    def wait(ref, sem):
        pltpu.make_async_copy(ref, ref, sem).wait()

    barrier = pltpu.get_barrier_semaphore()
    peers = [col_peer(k)[1] for k in range(1, outer)] + [row_peer(n, k)[1] for n, k in row_offsets]
    peers += [other_peer(n, k) for n, k in other_offsets]
    for device in peers:
        pl.semaphore_signal(barrier, inc=1, device_id=device, device_id_type=MESH)

    cuts = depths(feats)
    loads = [(cap_hbm, cap_v), (clip_hbm, clip_v)]
    loads += [(proj_hbm.at[cut], proj_v.at[cut]) for cut in cuts] + [(perm_hbm, perm_v)]
    loads = [pltpu.make_async_copy(src, dst, load_sem.at[n]) for n, (src, dst) in enumerate(loads)]
    for load in loads:
        load.start()
    loads[0].wait()
    raw_cap = cap_v[...].astype(f32)
    cap_inv = inverse_norm(raw_cap)
    unit_cap = raw_cap * cap_inv
    caps[c, z] = unit_cap.astype(bf16)
    loads[1].wait()
    part = None
    for n, cut in enumerate(cuts):
        loads[2 + n].wait()
        term = jnp.dot(clip_v[:, cut], proj_v[cut], preferred_element_type=f32)
        part = term if part is None else part + term
    part_own[...] = part
    part_send[...] = part.astype(bf16)
    pl.semaphore_wait(barrier, len(peers))
    own_caps = caps.at[c, z]
    far_first = sorted(range(1, outer), key=lambda k: -min(k, outer - k))
    for k in far_first:
        send(0, own_caps, own_caps, caps_rs.at[k - 1], col_peer(k)[1])
    if pair > 1:
        send(1, own_caps, own_caps, fwd_rs.at[0], core_peer)
    n1 = nq - direct(nq, nb)
    for q in range(n1):
        for k in range(1, tensor):
            send(2, part_send.at[pieces[q]], part_recv.at[k - 1, pieces[q]], part_rs.at[q], row_peer(0, k)[1])
    if n1 < nq:
        rest = pl.ds(n1 * step, rows - n1 * step)
        for n, k in row_offsets:
            place = n * tensor + k - 1
            send(3, part_send.at[rest], part_dir.at[place], part_dir_rs.at[0], row_peer(n, k)[1])
    cap_unit[...] = unit_cap
    loads[-1].wait()
    logit = logit_ref[0]

    vid_inv = [None] * nq
    for q in range(n1):
        piece = pieces[q]
        raw_proj = part_own[piece]
        if tensor > 1:
            wait(part_recv.at[:, piece], part_rs.at[q])
        for k in range(1, tensor):
            raw_proj = raw_proj + part_recv[k - 1, piece].astype(f32)
        vid_inv[q] = inverse_norm(raw_proj)
        unit = raw_proj * vid_inv[q]
        unit_vid[piece] = unit
        vids[c, i, piece] = unit.astype(bf16)
        for n in range(1, inner):
            here = vids.at[c, i, piece]
            send(4, here, here, vids_rs.at[n - 1, q], row_peer(n, 0)[1])
    for k in far_first[::-1][:-1]:
        pz = lax.rem(z + (outer - k), outer)
        wait(caps.at[c, pz], caps_rs.at[k - 1])
        if pair > 1:
            send(1, caps.at[c, pz], caps.at[c, pz], fwd_rs.at[k], core_peer)
    if n1 < nq:
        wait(part_dir, part_dir_rs.at[0])
        for n in range(inner):
            places = [n * tensor + k - 1 for k in range(tensor) if n or k]
            pi = lax.rem(i + (inner - n), inner)
            raw_proj = functools.reduce(
                jnp.add, ([] if n else [part_own[rest]]) + [part_dir[p].astype(f32) for p in places]
            )
            inverse = inverse_norm(raw_proj)
            unit = raw_proj * inverse
            vids[c, pi, rest] = unit.astype(bf16)
            if n == 0:
                unit_vid[rest] = unit
                for q in range(n1, nq):
                    vid_inv[q] = inverse[(q - n1) * step : (q - n1 + 1) * step]
    for k in far_first[:1]:
        pz = lax.rem(z + (outer - k), outer)
        wait(caps.at[c, pz], caps_rs.at[k - 1])
        if pair > 1:
            send(1, caps.at[c, pz], caps.at[c, pz], fwd_rs.at[k], core_peer)
    for n in range(1, inner):
        pi = lax.rem(i + (inner - n), inner)
        for q in range(n1):
            wait(vids.at[c, pi, pieces[q]], vids_rs.at[n - 1, q])

    if pair > 1:
        send(6, vids.at[c], vids.at[c], cross_rs.at[0], core_peer)
    half = outer * ccol
    index = lax.broadcasted_iota(jnp.int32, (half, 1), 0)

    def score(cc, rc):
        columns = caps[cc].reshape(half, width)
        videos = vids[rc].reshape(tile_rows, width)
        values = logit * lax.dot_general(columns, videos, (((1,), (1,)), ((), ())), preferred_element_type=f32)
        wanted = jnp.concatenate(
            [perm_v[:, pl.ds(pl.multiple_of(dp_index(z, n, rc) * rows, rows), rows)] for n in range(inner)], axis=1
        )
        return values, (dp_index(index // ccol, i, cc) * tensor + t) * ccol + index % ccol == wanted

    tiles = [score(c, c)]
    if pair > 1:
        for k in range(outer):
            pz = lax.rem(z + (outer - k), outer)
            wait(caps.at[1 - c, pz], fwd_rs.at[k])
        tiles.append(score(1 - c, c))
    top = functools.reduce(jnp.maximum, [jnp.max(v, axis=0, keepdims=True) for v, _ in tiles])
    expo = [jnp.exp(tile[0] - top) for tile in tiles]
    total = functools.reduce(jnp.add, [jnp.sum(v, axis=0, keepdims=True) for v in expo])
    positive = functools.reduce(jnp.add, [jnp.sum(jnp.where(h, v, 0.0), axis=0, keepdims=True) for v, h in tiles])
    stats[...] = jnp.concatenate([top, total, positive], axis=1)
    for n, k in row_offsets:
        send(5, stats, stats_recv.at[n * tensor + k - 1], stats_rs.at[0], row_peer(n, k)[1])
    for n, k in other_offsets:
        send(5, stats, stats_recv.at[nb - 1 + n * tensor + k], stats_rs.at[0], other_peer(n, k))
    if pair > 1:
        wait(vids.at[1 - c], cross_rs.at[0])
        cross, cross_hit = score(c, 1 - c)
    if pair * nb > 1:
        wait(stats_recv, stats_rs.at[0])

    def combine(every):
        tops = [v[:, :tile_rows] for v in every]
        row_max = functools.reduce(jnp.maximum, tops)
        sums = [v[:, tile_rows : 2 * tile_rows] * jnp.exp(m - row_max) for v, m in zip(every, tops)]
        return row_max, functools.reduce(jnp.add, sums)

    every = [stats[...]] + [stats_recv[n] for n in range(nb - 1)]
    row_max, row_sum = combine(every)
    row_pos = functools.reduce(jnp.add, [v[:, 2 * tile_rows :] for v in every])
    scale = jnp.exp(top - row_max) / row_sum
    weights = [(v * scale - tile[1].astype(f32)).astype(bf16) for v, tile in zip(expo, tiles)]

    def vid_rows(pi):
        cols = pl.ds(pl.multiple_of(pi * rows, rows), rows)
        terms = [
            lax.dot_general(
                weights_v[n, :, cols], caps[cc].reshape(half, width), (((0,), (0,)), ((), ())), preferred_element_type=f32
            )
            for n, cc in enumerate((c, 1 - c)[:pair])
        ]
        return functools.reduce(jnp.add, terms)

    for n, v in enumerate(weights):
        weights_v[n] = v
    n2 = nq - direct_back(nq, nb)
    rest = pl.ds(n2 * step, rows - n2 * step)
    for n in range(1, inner):
        pi, dev = row_peer(n, 0)
        row_send[pi] = vid_rows(pi).astype(bf16)
        for q in range(n2):
            send(7, row_send.at[pi, pieces[q]], row_recv.at[n - 1, pieces[q]], row_rs.at[n - 1, q], dev)
    own = jnp.dot(weights[0], vids[c].reshape(tile_rows, width), preferred_element_type=f32)
    if pair > 1:
        cross_max, cross_sum = combine([stats_recv[nb - 1 + n] for n in range(nb)])
        cross = (jnp.exp(cross - cross_max) / cross_sum - cross_hit.astype(f32)).astype(bf16)
        own = own + jnp.dot(cross, vids[1 - c].reshape(tile_rows, width), preferred_element_type=f32)
    cap_acc[...] = own.reshape(outer, ccol, width)
    for k in far_first:
        pz, dev = col_peer(k)
        cap_send[k - 1] = cap_acc[pz].astype(bf16)
        send(9, cap_send.at[k - 1], cap_recv.at[k - 1], cg_rs.at[k - 1], dev)
    own_rows = vid_rows(i)
    row_part[...] = own_rows
    if n2 < nq:
        row_send[i, rest] = own_rows[n2 * step :].astype(bf16)
        for n, k in row_offsets:
            pi, dev = row_peer(n, k)
            send(8, row_send.at[pi, rest], row_dir.at[n * tensor + k - 1], row_dir_rs.at[0], dev)
    loss_v[...] = row_max + jnp.log(row_sum) - row_pos
    loss_ref[...] = loss_v[:, pl.ds(pl.multiple_of(i * rows, rows), rows)]

    def clip_rows(piece, vid_grad, inverse):
        vid_grad = logit * vid_grad
        unit = unit_vid[piece]
        vid_dot = jnp.sum(unit * vid_grad, axis=1, keepdims=True)
        raw_grad = ((vid_grad - unit * vid_dot) * inverse).astype(bf16)
        clip_grad_ref[piece] = lax.dot_general(
            raw_grad, proj_v[...], (((1,), (1,)), ((), ())), preferred_element_type=f32
        )

    for q in range(n2):
        piece = pieces[q]
        piece_sum = row_part[piece]
        for n in range(1, inner):
            wait(row_recv.at[n - 1, piece], row_rs.at[n - 1, q])
            piece_sum = piece_sum + row_recv[n - 1, piece].astype(f32)
        row_part[piece] = piece_sum
        sum_send[piece] = piece_sum.astype(bf16)
        for k in range(1, tensor):
            send(10, sum_send.at[piece], sum_recv.at[k - 1, piece], sum_rs.at[q], row_peer(0, k)[1])
    if n2 < nq:
        wait(row_dir, row_dir_rs.at[0])
        vid_grad = functools.reduce(jnp.add, [row_part[rest]] + [row_dir[n].astype(f32) for n in range(nb - 1)])
        clip_rows(rest, vid_grad, jnp.concatenate(vid_inv[n2:], axis=0))
    for q in range(n2):
        piece = pieces[q]
        vid_grad = row_part[piece]
        if tensor > 1:
            wait(sum_recv.at[:, piece], sum_rs.at[q])
        for k in range(1, tensor):
            vid_grad = vid_grad + sum_recv[k - 1, piece].astype(f32)
        clip_rows(piece, vid_grad, vid_inv[q])
    cap_grad = cap_acc[z]
    for k in reversed(far_first):
        wait(cap_recv.at[k - 1], cg_rs.at[k - 1])
        cap_grad = cap_grad + cap_recv[k - 1].astype(f32)
    cap_grad = logit * cap_grad
    unit = cap_unit[...]
    cap_dot = jnp.sum(unit * cap_grad, axis=1, keepdims=True)
    cap_grad_ref[...] = (cap_grad - unit * cap_dot) * cap_inv
    for group, refs in sent.items():
        for ref in refs:
            wait(ref, send_sem.at[group])


def store_kernel(*refs):
    count = len(refs) // 2
    sems = refs[-1]
    copies = [pltpu.make_async_copy(refs[n], refs[count + n], sems.at[n]) for n in range(count)]
    for copy in copies:
        copy.start()
    for copy in copies:
        copy.wait()


def store_results(*values):
    return pl.pallas_call(
        store_kernel,
        out_shape=tuple(jax.ShapeDtypeStruct(v.shape, v.dtype) for v in values),
        in_specs=[pl.BlockSpec(memory_space=pltpu.VMEM)] * len(values),
        out_specs=tuple(pl.BlockSpec(memory_space=pltpu.HBM) for v in values),
        scratch_shapes=[pltpu.SemaphoreType.DMA((len(values),))],
        compiler_params=pltpu.CompilerParams(vmem_limit_bytes=4 * 1024 * 1024),
        name="store_results",
    )(*values)


def body(dp, tensor, clip_feats, proj_weight, caption_emb, logit_scale, pair_perm):
    rows, feats = clip_feats.shape
    ccol, width = caption_emb.shape
    outer, inner, pair = split(dp)
    nb = inner * tensor
    tile_rows = inner * rows
    nq = chunks(rows)
    vmem = pl.BlockSpec(memory_space=pltpu.VMEM)
    hbm = pl.BlockSpec(memory_space=pltpu.HBM)
    dma = pltpu.SemaphoreType.DMA
    nr, no, nt, ni = max(nb - 1, 1), max(outer - 1, 1), max(tensor - 1, 1), max(inner - 1, 1)
    nd1 = direct(nq, nb)
    nd2 = direct_back(nq, nb)
    clip_grad, caption_grad, losses = pl.pallas_call(
        functools.partial(kernel, dp, tensor),
        out_shape=(
            jax.ShapeDtypeStruct((rows, feats), f32),
            jax.ShapeDtypeStruct((ccol, width), f32),
            jax.ShapeDtypeStruct((1, rows), f32),
        ),
        in_specs=[pl.BlockSpec(memory_space=pltpu.SMEM)] + [hbm] * 4,
        out_specs=(vmem, vmem, vmem),
        scratch_shapes=[
            pltpu.VMEM((1, pair_perm.shape[0]), jnp.int32),
            pltpu.VMEM((rows, feats), bf16),
            pltpu.VMEM(proj_weight.shape, bf16),
            pltpu.VMEM((rows, width), f32),
            pltpu.VMEM((rows, width), bf16),
            pltpu.VMEM((nt, rows, width), bf16),
            pltpu.VMEM((nr, max(nd1, 1) * (rows // nq), width), bf16),
            pltpu.VMEM((rows, width), f32),
            pltpu.VMEM((ccol, width), bf16),
            pltpu.VMEM((pair, outer, ccol, width), bf16),
            pltpu.VMEM((ccol, width), f32),
            pltpu.VMEM((pair, inner, rows, width), bf16),
            pltpu.VMEM((1, 3 * tile_rows), f32),
            pltpu.VMEM((max(pair * nb - 1, 1), 1, 3 * tile_rows), f32),
            pltpu.VMEM((1, tile_rows), f32),
            pltpu.VMEM((pair, outer * ccol, tile_rows), bf16),
            pltpu.VMEM((outer, ccol, width), f32),
            pltpu.VMEM((rows, width), f32),
            pltpu.VMEM((inner, rows, width), bf16),
            pltpu.VMEM((ni, rows, width), bf16),
            pltpu.VMEM((nr, max(nd2, 1) * (rows // nq), width), bf16),
            pltpu.VMEM((rows, width), bf16),
            pltpu.VMEM((nt, rows, width), bf16),
            pltpu.VMEM((no, ccol, width), bf16),
            pltpu.VMEM((no, ccol, width), bf16),
            dma((len(depths(feats)) + 3,)),
            dma((11,)),
            dma((max(nq - nd1, 1),)),
            dma((1,)),
            dma((no,)),
            dma((outer,)),
            dma((ni, max(nq - nd1, 1))),
            dma((1,)),
            dma((ni, nq)),
            dma((1,)),
            dma((nq,)),
            dma((1,)),
            dma((no,)),
        ],
        compiler_params=pltpu.CompilerParams(collective_id=0, has_side_effects=True, vmem_limit_bytes=48 * 1024 * 1024),
        name="contrastive_step",
    )(
        logit_scale,
        *[
            pltpu.with_memory_space_constraint(x, pltpu.HBM)
            for x in (pair_perm.reshape(1, -1), clip_feats, proj_weight, caption_emb)
        ]
    )
    clip_grad, caption_grad, losses = store_results(clip_grad, caption_grad, losses)
    return clip_grad, caption_grad, losses.reshape(rows)


def solution(mesh):
    return jax.shard_map(
        functools.partial(body, mesh.shape["dp"], mesh.shape["tensor"]),
        mesh=mesh,
        in_specs=(P("dp", "tensor"), P("tensor", None), P(("dp", "tensor"), None), P(), P()),
        out_specs=(P("dp", "tensor"), P(("dp", "tensor"), None), P("dp")),
        check_vma=False,
    )
```

```python
import functools

import jax
import jax.numpy as jnp
from jax import lax
from jax.experimental import pallas as pl
from jax.experimental.pallas import tpu as pltpu
from jax.sharding import PartitionSpec as P

norm_eps = 1e-06
MESH = pl.DeviceIdType.MESH
f32 = jnp.float32
bf16 = jnp.bfloat16


def split(dp):
    pair = 2 if dp % 2 == 0 else 1
    rest = dp // pair
    inner = max(n for n in range(1, rest + 1) if rest % n == 0 and n * n <= rest)
    return rest // inner, inner, pair


def chunks(rows):
    return max(n for n in (1, 2, 4) if rows % (16 * n) == 0 or n == 1)


def direct(nq, nb):
    return nq // 2 if nb > 1 else 0


def direct_back(nq, nb):
    return 2 * nq // 4 if nb > 1 else 0


def depths(feats):
    size = 256 if feats > 256 else feats
    return [pl.ds(n, min(size, feats - n)) for n in range(0, feats, size)]


def inverse_norm(values):
    return lax.rsqrt(jnp.sum(values * values, axis=1, keepdims=True) + norm_eps)


def kernel(
    dp,
    tensor,
    logit_ref,
    perm_hbm,
    clip_hbm,
    proj_hbm,
    cap_hbm,
    clip_grad_ref,
    cap_grad_ref,
    loss_ref,
    perm_v,
    clip_v,
    proj_v,
    proj_t,
    part_own,
    part_send,
    part_recv,
    part_dir,
    unit_vid,
    cap_v,
    caps,
    cap_unit,
    vids,
    stats,
    stats_recv,
    loss_v,
    weights_v,
    cap_acc,
    row_part,
    row_send,
    row_recv,
    row_dir,
    sum_send,
    sum_recv,
    cap_send,
    cap_recv,
    load_sem,
    send_sem,
    part_rs,
    part_dir_rs,
    caps_rs,
    fwd_rs,
    vids_rs,
    stats_rs,
    row_rs,
    row_dir_rs,
    sum_rs,
    cross_rs,
    cg_rs,
):
    outer, inner, pair = split(dp)
    nb = inner * tensor
    rows, feats = clip_v.shape
    ccol, width = cap_hbm.shape
    tile_cols = outer * pair * ccol
    tile_rows = inner * rows
    nq = chunks(rows)
    step = rows // nq
    pieces = [pl.ds(q * step, step) for q in range(nq)]
    d = lax.axis_index("dp")
    t = lax.axis_index("tensor")
    c = lax.rem(d, pair)
    i = lax.rem(lax.div(d, pair), inner)
    z = lax.div(d, pair * inner)

    def dp_index(zz, ii, cc):
        return (zz * inner + ii) * pair + cc

    row_offsets = [(n, k) for n in range(inner) for k in range(tensor) if n or k]
    other_offsets = [(n, k) for n in range(inner) for k in range(tensor)] if pair > 1 else []

    def row_peer(n, k):
        pi = lax.rem(i + n, inner)
        return pi, (dp_index(z, pi, c), lax.rem(t + k, tensor))

    def other_peer(n, k):
        return (dp_index(z, lax.rem(i + n, inner), pair - 1 - c), lax.rem(t + k, tensor))

    def col_peer(k):
        pz = lax.rem(z + k, outer)
        return pz, (dp_index(pz, i, c), t)

    core_peer = (dp_index(z, i, pair - 1 - c), t)
    sent = []

    def send(src, dst, rs, device):
        copy = pltpu.make_async_remote_copy(
            src_ref=src, dst_ref=dst, send_sem=send_sem.at[0], recv_sem=rs, device_id=device, device_id_type=MESH
        )
        copy.start()
        sent.append(src)

    def wait(ref, sem):
        pltpu.make_async_copy(ref, ref, sem).wait()

    barrier = pltpu.get_barrier_semaphore()
    peers = [col_peer(k)[1] for k in range(1, outer)] + [row_peer(n, k)[1] for n, k in row_offsets]
    peers += [other_peer(n, k) for n, k in other_offsets]
    for device in peers:
        pl.semaphore_signal(barrier, inc=1, device_id=device, device_id_type=MESH)

    cuts = depths(feats)
    loads = [(cap_hbm, cap_v), (clip_hbm, clip_v)]
    loads += [(proj_hbm.at[cut], proj_v.at[cut]) for cut in cuts] + [(perm_hbm, perm_v)]
    loads = [pltpu.make_async_copy(src, dst, load_sem.at[n]) for n, (src, dst) in enumerate(loads)]
    for load in loads:
        load.start()
    loads[0].wait()
    raw_cap = cap_v[...].astype(f32)
    cap_inv = inverse_norm(raw_cap)
    unit_cap = raw_cap * cap_inv
    caps[c, z] = unit_cap.astype(bf16)
    loads[1].wait()
    part = None
    for n, cut in enumerate(cuts):
        loads[2 + n].wait()
        term = jnp.dot(clip_v[:, cut], proj_v[cut], preferred_element_type=f32)
        part = term if part is None else part + term
    part_own[...] = part
    part_send[...] = part.astype(bf16)
    pl.semaphore_wait(barrier, len(peers))
    own_caps = caps.at[c, z]
    far_first = sorted(range(1, outer), key=lambda k: -min(k, outer - k))
    for k in far_first:
        send(own_caps, own_caps, caps_rs.at[k - 1], col_peer(k)[1])
    if pair > 1:
        send(own_caps, own_caps, fwd_rs.at[0], core_peer)
    n1 = nq - direct(nq, nb)
    for q in range(n1):
        for k in range(1, tensor):
            send(part_send.at[pieces[q]], part_recv.at[k - 1, pieces[q]], part_rs.at[q], row_peer(0, k)[1])
    proj_t[...] = proj_v[...].T
    if n1 < nq:
        rest = pl.ds(n1 * step, rows - n1 * step)
        for n, k in row_offsets:
            place = n * tensor + k - 1
            send(part_send.at[rest], part_dir.at[place], part_dir_rs.at[0], row_peer(n, k)[1])
    cap_unit[...] = unit_cap
    loads[-1].wait()
    logit = logit_ref[0]

    vid_inv = [None] * nq
    for q in range(n1):
        piece = pieces[q]
        raw_proj = part_own[piece]
        if tensor > 1:
            wait(part_recv.at[:, piece], part_rs.at[q])
        for k in range(1, tensor):
            raw_proj = raw_proj + part_recv[k - 1, piece].astype(f32)
        vid_inv[q] = inverse_norm(raw_proj)
        unit = raw_proj * vid_inv[q]
        unit_vid[piece] = unit
        vids[c, i, piece] = unit.astype(bf16)
        for n in range(1, inner):
            here = vids.at[c, i, piece]
            send(here, here, vids_rs.at[n - 1], row_peer(n, 0)[1])
    for k in far_first[::-1][:-1]:
        pz = lax.rem(z + (outer - k), outer)
        wait(caps.at[c, pz], caps_rs.at[k - 1])
        if pair > 1:
            send(caps.at[c, pz], caps.at[c, pz], fwd_rs.at[0], core_peer)
    if n1 < nq:
        wait(part_dir, part_dir_rs.at[0])
        for n in range(inner):
            places = [n * tensor + k - 1 for k in range(tensor) if n or k]
            pi = lax.rem(i + (inner - n), inner)
            raw_proj = functools.reduce(
                jnp.add, ([] if n else [part_own[rest]]) + [part_dir[p].astype(f32) for p in places]
            )
            inverse = inverse_norm(raw_proj)
            unit = raw_proj * inverse
            vids[c, pi, rest] = unit.astype(bf16)
            if n == 0:
                unit_vid[rest] = unit
                for q in range(n1, nq):
                    vid_inv[q] = inverse[(q - n1) * step : (q - n1 + 1) * step]
    for k in far_first[:1]:
        pz = lax.rem(z + (outer - k), outer)
        wait(caps.at[c, pz], caps_rs.at[k - 1])
        if pair > 1:
            send(caps.at[c, pz], caps.at[c, pz], fwd_rs.at[0], core_peer)
    for n in range(1, inner):
        pi = lax.rem(i + (inner - n), inner)
        wait(vids.at[c, pi, pl.ds(0, n1 * step)], vids_rs.at[n - 1])

    if pair > 1:
        send(vids.at[c], vids.at[c], cross_rs.at[0], core_peer)
    half = outer * ccol
    index = lax.broadcasted_iota(jnp.int32, (half, 1), 0)

    def score(cc, rc):
        columns = caps[cc].reshape(half, width)
        videos = vids[rc].reshape(tile_rows, width)
        values = logit * lax.dot_general(columns, videos, (((1,), (1,)), ((), ())), preferred_element_type=f32)
        wanted = jnp.concatenate(
            [perm_v[:, pl.ds(pl.multiple_of(dp_index(z, n, rc) * rows, rows), rows)] for n in range(inner)], axis=1
        )
        return values, (dp_index(index // ccol, i, cc) * tensor + t) * ccol + index % ccol == wanted

    tiles = [score(c, c)]
    if pair > 1:
        wait(caps.at[1 - c], fwd_rs.at[0])
        tiles.append(score(1 - c, c))
    top = functools.reduce(jnp.maximum, [jnp.max(v, axis=0, keepdims=True) for v, _ in tiles])
    expo = [jnp.exp(tile[0] - top) for tile in tiles]
    total = functools.reduce(jnp.add, [jnp.sum(v, axis=0, keepdims=True) for v in expo])
    positive = functools.reduce(jnp.add, [jnp.sum(jnp.where(h, v, 0.0), axis=0, keepdims=True) for v, h in tiles])
    stats[...] = jnp.concatenate([top, total, positive], axis=1)
    for n, k in row_offsets:
        send(stats, stats_recv.at[n * tensor + k - 1], stats_rs.at[0], row_peer(n, k)[1])
    for n, k in other_offsets:
        send(stats, stats_recv.at[nb - 1 + n * tensor + k], stats_rs.at[0], other_peer(n, k))
    if pair > 1:
        wait(vids.at[1 - c], cross_rs.at[0])
        cross, cross_hit = score(c, 1 - c)
    if pair * nb > 1:
        wait(stats_recv, stats_rs.at[0])

    def combine(every):
        tops = [v[:, :tile_rows] for v in every]
        row_max = functools.reduce(jnp.maximum, tops)
        sums = [v[:, tile_rows : 2 * tile_rows] * jnp.exp(m - row_max) for v, m in zip(every, tops)]
        return row_max, functools.reduce(jnp.add, sums)

    every = [stats[...]] + [stats_recv[n] for n in range(nb - 1)]
    row_max, row_sum = combine(every)
    row_pos = functools.reduce(jnp.add, [v[:, 2 * tile_rows :] for v in every])
    scale = jnp.exp(top - row_max) / row_sum
    weights = [(v * scale - tile[1].astype(f32)).astype(bf16) for v, tile in zip(expo, tiles)]

    def vid_rows(pi):
        cols = pl.ds(pl.multiple_of(pi * rows, rows), rows)
        terms = [
            lax.dot_general(
                weights_v[n, :, cols], caps[cc].reshape(half, width), (((0,), (0,)), ((), ())), preferred_element_type=f32
            )
            for n, cc in enumerate((c, 1 - c)[:pair])
        ]
        return functools.reduce(jnp.add, terms)

    for n, v in enumerate(weights):
        weights_v[n] = v
    n2 = nq - direct_back(nq, nb)
    rest = pl.ds(n2 * step, rows - n2 * step)
    for n in range(1, inner):
        pi, dev = row_peer(n, 0)
        row_send[pi] = vid_rows(pi).astype(bf16)
        for q in range(n2):
            send(row_send.at[pi, pieces[q]], row_recv.at[n - 1, pieces[q]], row_rs.at[n - 1, q], dev)
    own = jnp.dot(weights[0], vids[c].reshape(tile_rows, width), preferred_element_type=f32)
    if pair > 1:
        cross_max, cross_sum = combine([stats_recv[nb - 1 + n] for n in range(nb)])
        cross = (jnp.exp(cross - cross_max) / cross_sum - cross_hit.astype(f32)).astype(bf16)
        own = own + jnp.dot(cross, vids[1 - c].reshape(tile_rows, width), preferred_element_type=f32)
    cap_acc[...] = own.reshape(outer, ccol, width)
    for k in far_first:
        pz, dev = col_peer(k)
        cap_send[k - 1] = cap_acc[pz].astype(bf16)
        send(cap_send.at[k - 1], cap_recv.at[k - 1], cg_rs.at[0], dev)
    own_rows = vid_rows(i)
    row_part[...] = own_rows
    if n2 < nq:
        row_send[i, rest] = own_rows[n2 * step :].astype(bf16)
        for n, k in row_offsets:
            pi, dev = row_peer(n, k)
            send(row_send.at[pi, rest], row_dir.at[n * tensor + k - 1], row_dir_rs.at[0], dev)
    loss_v[...] = row_max + jnp.log(row_sum) - row_pos
    loss_ref[...] = loss_v[:, pl.ds(pl.multiple_of(i * rows, rows), rows)]

    def clip_rows(piece, vid_grad, inverse):
        vid_grad = logit * vid_grad
        unit = unit_vid[piece]
        vid_dot = jnp.sum(unit * vid_grad, axis=1, keepdims=True)
        raw_grad = ((vid_grad - unit * vid_dot) * inverse).astype(bf16)
        clip_grad_ref[piece] = jnp.dot(raw_grad, proj_t[...], preferred_element_type=f32)

    for q in range(n2):
        piece = pieces[q]
        piece_sum = row_part[piece]
        for n in range(1, inner):
            wait(row_recv.at[n - 1, piece], row_rs.at[n - 1, q])
            piece_sum = piece_sum + row_recv[n - 1, piece].astype(f32)
        row_part[piece] = piece_sum
        sum_send[piece] = piece_sum.astype(bf16)
        for k in range(1, tensor):
            send(sum_send.at[piece], sum_recv.at[k - 1, piece], sum_rs.at[q], row_peer(0, k)[1])
    for q in range(n2):
        if q == min(1, n2 - 1) and n2 < nq:
            wait(row_dir, row_dir_rs.at[0])
            vid_grad = functools.reduce(jnp.add, [row_part[rest]] + [row_dir[n].astype(f32) for n in range(nb - 1)])
            clip_rows(rest, vid_grad, jnp.concatenate(vid_inv[n2:], axis=0))
        piece = pieces[q]
        vid_grad = row_part[piece]
        if tensor > 1:
            wait(sum_recv.at[:, piece], sum_rs.at[q])
        for k in range(1, tensor):
            vid_grad = vid_grad + sum_recv[k - 1, piece].astype(f32)
        clip_rows(piece, vid_grad, vid_inv[q])
    cap_grad = cap_acc[z]
    if outer > 1:
        wait(cap_recv, cg_rs.at[0])
    for k in range(1, outer):
        cap_grad = cap_grad + cap_recv[k - 1].astype(f32)
    cap_grad = logit * cap_grad
    unit = cap_unit[...]
    cap_dot = jnp.sum(unit * cap_grad, axis=1, keepdims=True)
    cap_grad_ref[...] = (cap_grad - unit * cap_dot) * cap_inv
    for ref in sent:
        wait(ref, send_sem.at[0])


def store_kernel(*refs):
    count = len(refs) // 2
    sems = refs[-1]
    copies = [pltpu.make_async_copy(refs[n], refs[count + n], sems.at[n]) for n in range(count)]
    for copy in copies:
        copy.start()
    for copy in copies:
        copy.wait()


def store_results(*values):
    return pl.pallas_call(
        store_kernel,
        out_shape=tuple(jax.ShapeDtypeStruct(v.shape, v.dtype) for v in values),
        in_specs=[pl.BlockSpec(memory_space=pltpu.VMEM)] * len(values),
        out_specs=tuple(pl.BlockSpec(memory_space=pltpu.HBM) for v in values),
        scratch_shapes=[pltpu.SemaphoreType.DMA((len(values),))],
        compiler_params=pltpu.CompilerParams(vmem_limit_bytes=4 * 1024 * 1024),
        name="store_results",
    )(*values)


def body(dp, tensor, clip_feats, proj_weight, caption_emb, logit_scale, pair_perm):
    rows, feats = clip_feats.shape
    ccol, width = caption_emb.shape
    outer, inner, pair = split(dp)
    nb = inner * tensor
    tile_rows = inner * rows
    nq = chunks(rows)
    vmem = pl.BlockSpec(memory_space=pltpu.VMEM)
    hbm = pl.BlockSpec(memory_space=pltpu.HBM)
    dma = pltpu.SemaphoreType.DMA
    nr, no, nt, ni = max(nb - 1, 1), max(outer - 1, 1), max(tensor - 1, 1), max(inner - 1, 1)
    nd1 = direct(nq, nb)
    nd2 = direct_back(nq, nb)
    clip_grad, caption_grad, losses = pl.pallas_call(
        functools.partial(kernel, dp, tensor),
        out_shape=(
            jax.ShapeDtypeStruct((rows, feats), f32),
            jax.ShapeDtypeStruct((ccol, width), f32),
            jax.ShapeDtypeStruct((1, rows), f32),
        ),
        in_specs=[pl.BlockSpec(memory_space=pltpu.SMEM)] + [hbm] * 4,
        out_specs=(vmem, vmem, vmem),
        scratch_shapes=[
            pltpu.VMEM((1, pair_perm.shape[0]), jnp.int32),
            pltpu.VMEM((rows, feats), bf16),
            pltpu.VMEM(proj_weight.shape, bf16),
            pltpu.VMEM(proj_weight.shape[::-1], bf16),
            pltpu.VMEM((rows, width), f32),
            pltpu.VMEM((rows, width), bf16),
            pltpu.VMEM((nt, rows, width), bf16),
            pltpu.VMEM((nr, max(nd1, 1) * (rows // nq), width), bf16),
            pltpu.VMEM((rows, width), f32),
            pltpu.VMEM((ccol, width), bf16),
            pltpu.VMEM((pair, outer, ccol, width), bf16),
            pltpu.VMEM((ccol, width), f32),
            pltpu.VMEM((pair, inner, rows, width), bf16),
            pltpu.VMEM((1, 3 * tile_rows), f32),
            pltpu.VMEM((max(pair * nb - 1, 1), 1, 3 * tile_rows), f32),
            pltpu.VMEM((1, tile_rows), f32),
            pltpu.VMEM((pair, outer * ccol, tile_rows), bf16),
            pltpu.VMEM((outer, ccol, width), f32),
            pltpu.VMEM((rows, width), f32),
            pltpu.VMEM((inner, rows, width), bf16),
            pltpu.VMEM((ni, rows, width), bf16),
            pltpu.VMEM((nr, max(nd2, 1) * (rows // nq), width), bf16),
            pltpu.VMEM((rows, width), bf16),
            pltpu.VMEM((nt, rows, width), bf16),
            pltpu.VMEM((no, ccol, width), bf16),
            pltpu.VMEM((no, ccol, width), bf16),
            dma((len(depths(feats)) + 3,)),
            dma((1,)),
            dma((nq - nd1,)),
            dma((1,)),
            dma((no,)),
            dma((1,)),
            dma((ni,)),
            dma((2,)),
            dma((ni, nq - nd2)),
            dma((1,)),
            dma((nq - nd2,)),
            dma((1,)),
            dma((1,)),
        ],
        compiler_params=pltpu.CompilerParams(collective_id=0, has_side_effects=True, vmem_limit_bytes=48 * 1024 * 1024),
        name="contrastive_step",
    )(
        logit_scale,
        *[
            pltpu.with_memory_space_constraint(x, pltpu.HBM)
            for x in (pair_perm.reshape(1, -1), clip_feats, proj_weight, caption_emb)
        ]
    )
    clip_grad, caption_grad, losses = store_results(clip_grad, caption_grad, losses)
    return clip_grad, caption_grad, losses.reshape(rows)


def solution(mesh):
    return jax.shard_map(
        functools.partial(body, mesh.shape["dp"], mesh.shape["tensor"]),
        mesh=mesh,
        in_specs=(P("dp", "tensor"), P("tensor", None), P(("dp", "tensor"), None), P(), P()),
        out_specs=(P("dp", "tensor"), P(("dp", "tensor"), None), P("dp")),
        check_vma=False,
    )
```

```python
import functools

import jax
import jax.numpy as jnp
from jax import lax
from jax.experimental import pallas as pl
from jax.experimental.pallas import tpu as pltpu
from jax.sharding import PartitionSpec as P

norm_eps = 1e-06
MESH = pl.DeviceIdType.MESH
f32 = jnp.float32
bf16 = jnp.bfloat16


def split(dp):
    pair = 2 if dp % 2 == 0 else 1
    rest = dp // pair
    inner = max(n for n in range(1, rest + 1) if rest % n == 0 and n * n <= rest)
    return rest // inner, inner, pair


def pieces_of(rows, nb, eighths):
    if nb == 1 or rows % 128:
        return [(0, rows)], 0
    cuts = [sum(eighths[:n]) * rows // 8 for n in range(len(eighths) + 1)]
    return [(a, b - a) for a, b in zip(cuts, cuts[1:])], rows - cuts[-1]


forward, backward = (2,2), (2,2)


def depths(feats):
    size = 256 if feats > 256 else feats
    return [pl.ds(n, min(size, feats - n)) for n in range(0, feats, size)]


def inverse_norm(values):
    return lax.rsqrt(jnp.sum(values * values, axis=1, keepdims=True) + norm_eps)


def kernel(
    dp,
    tensor,
    logit_ref,
    perm_hbm,
    clip_hbm,
    proj_hbm,
    cap_hbm,
    clip_grad_ref,
    cap_grad_ref,
    loss_ref,
    perm_v,
    clip_v,
    proj_v,
    proj_t,
    part_own,
    part_send,
    part_recv,
    part_dir,
    unit_vid,
    inv_v,
    cap_v,
    caps,
    cap_unit,
    vids,
    stats,
    stats_recv,
    loss_v,
    weights_v,
    cap_acc,
    row_part,
    row_send,
    row_recv,
    row_dir,
    sum_send,
    sum_recv,
    cap_send,
    cap_recv,
    load_sem,
    send_sem,
    part_rs,
    part_dir_rs,
    caps_rs,
    fwd_rs,
    vids_rs,
    stats_rs,
    row_rs,
    row_dir_rs,
    sum_rs,
    cross_rs,
    cg_rs,
):
    outer, inner, pair = split(dp)
    nb = inner * tensor
    rows, feats = clip_v.shape
    ccol, width = cap_hbm.shape
    tile_cols = outer * pair * ccol
    tile_rows = inner * rows
    forth, part_rest = pieces_of(rows, nb, forward)
    back, row_rest = pieces_of(rows, nb, backward)
    d = lax.axis_index("dp")
    t = lax.axis_index("tensor")
    c = lax.rem(d, pair)
    i = lax.rem(lax.div(d, pair), inner)
    z = lax.div(d, pair * inner)

    def dp_index(zz, ii, cc):
        return (zz * inner + ii) * pair + cc

    row_offsets = [(n, k) for n in range(inner) for k in range(tensor) if n or k]
    other_offsets = [(n, k) for n in range(inner) for k in range(tensor)] if pair > 1 else []

    def row_peer(n, k):
        pi = lax.rem(i + n, inner)
        return pi, (dp_index(z, pi, c), lax.rem(t + k, tensor))

    def other_peer(n, k):
        return (dp_index(z, lax.rem(i + n, inner), pair - 1 - c), lax.rem(t + k, tensor))

    def col_peer(k):
        pz = lax.rem(z + k, outer)
        return pz, (dp_index(pz, i, c), t)

    core_peer = (dp_index(z, i, pair - 1 - c), t)
    peer = {(n, k): row_peer(n, k) for n in range(inner) for k in range(tensor)}
    source = [lax.rem(i + (inner - n), inner) for n in range(inner)]
    sent, sent_by = [], ([], [])

    def on_core(core):
        return pl.when(c == core)

    def send(src, dst, rs, device):
        copy = pltpu.make_async_remote_copy(
            src_ref=src, dst_ref=dst, send_sem=send_sem.at[0], recv_sem=rs, device_id=device, device_id_type=MESH
        )
        copy.start()
        sent.append(src)

    def send_on(core, src, dst, rs, device):
        copy = pltpu.make_async_remote_copy(
            src_ref=src, dst_ref=dst, send_sem=send_sem.at[0], recv_sem=rs, device_id=device, device_id_type=MESH
        )
        copy.start()
        sent_by[core].append(src)

    def wait(ref, sem):
        pltpu.make_async_copy(ref, ref, sem).wait()

    barrier = pltpu.get_barrier_semaphore()
    peers = [col_peer(k)[1] for k in range(1, outer)] + [row_peer(n, k)[1] for n, k in row_offsets]
    peers += [other_peer(n, k) for n, k in other_offsets]
    for device in peers:
        pl.semaphore_signal(barrier, inc=1, device_id=device, device_id_type=MESH)

    cuts = depths(feats)
    loads = [(cap_hbm, cap_v), (clip_hbm, clip_v)]
    loads += [(proj_hbm.at[cut], proj_v.at[cut]) for cut in cuts] + [(perm_hbm, perm_v)]
    loads = [pltpu.make_async_copy(src, dst, load_sem.at[n]) for n, (src, dst) in enumerate(loads)]
    for load in loads:
        load.start()
    loads[0].wait()
    raw_cap = cap_v[...].astype(f32)
    cap_inv = inverse_norm(raw_cap)
    unit_cap = raw_cap * cap_inv
    caps[c, z] = unit_cap.astype(bf16)
    loads[1].wait()
    part = None
    for n, cut in enumerate(cuts):
        loads[2 + n].wait()
        term = jnp.dot(clip_v[:, cut], proj_v[cut], preferred_element_type=f32)
        part = term if part is None else part + term
    part_own[...] = part
    part_send[...] = part.astype(bf16)
    pl.semaphore_wait(barrier, len(peers))
    own_caps = caps.at[c, z]
    far_first = sorted(range(1, outer), key=lambda k: -min(k, outer - k))
    for k in far_first:
        send(own_caps, own_caps, caps_rs.at[k - 1], col_peer(k)[1])
    if pair > 1:
        send(own_caps, own_caps, fwd_rs.at[0], core_peer)
    for q, (at, size) in enumerate(forth):
        piece = pl.ds(at, size)
        for k in range(1, tensor):
            send(part_send.at[piece], part_recv.at[k - 1, piece], part_rs.at[q], peer[0, k][1])
    proj_t[...] = proj_v[...].T
    if part_rest:
        rest = pl.ds(rows - part_rest, part_rest)
        for n, k in row_offsets:
            place = n * tensor + k - 1
            send(part_send.at[rest], part_dir.at[place], part_dir_rs.at[0], peer[n, k][1])
    cap_unit[...] = unit_cap
    loads[-1].wait()
    logit = logit_ref[0]

    for q, (at, size) in enumerate(forth):
        piece = pl.ds(at, size)
        raw_proj = part_own[piece]
        if tensor > 1:
            wait(part_recv.at[:, piece], part_rs.at[q])
        for k in range(1, tensor):
            raw_proj = raw_proj + part_recv[k - 1, piece].astype(f32)
        inverse = inverse_norm(raw_proj)
        inv_v[piece] = inverse
        unit = raw_proj * inverse
        unit_vid[piece] = unit
        vids[c, i, piece] = unit.astype(bf16)
        for n in range(1, inner):
            here = vids.at[c, i, piece]
            send(here, here, vids_rs.at[n - 1], peer[n, 0][1])
    for k in far_first[::-1][:-1]:
        pz = lax.rem(z + (outer - k), outer)
        wait(caps.at[c, pz], caps_rs.at[k - 1])
        if pair > 1:
            send(caps.at[c, pz], caps.at[c, pz], fwd_rs.at[0], core_peer)
    if part_rest:
        wait(part_dir, part_dir_rs.at[0])
        for n in range(inner):
            places = [n * tensor + k - 1 for k in range(tensor) if n or k]
            pi = source[n]
            raw_proj = functools.reduce(
                jnp.add, ([] if n else [part_own[rest]]) + [part_dir[p].astype(f32) for p in places]
            )
            inverse = inverse_norm(raw_proj)
            unit = raw_proj * inverse
            vids[c, pi, rest] = unit.astype(bf16)
            if n == 0:
                unit_vid[rest] = unit
                inv_v[rest] = inverse
    for k in far_first[:1]:
        pz = lax.rem(z + (outer - k), outer)
        wait(caps.at[c, pz], caps_rs.at[k - 1])
        if pair > 1:
            send(caps.at[c, pz], caps.at[c, pz], fwd_rs.at[0], core_peer)
    for n in range(1, inner):
        pi = source[n]
        wait(vids.at[c, pi, pl.ds(0, rows - part_rest)], vids_rs.at[n - 1])

    if pair > 1:
        send(vids.at[c], vids.at[c], cross_rs.at[0], core_peer)
    half = outer * ccol
    index = lax.broadcasted_iota(jnp.int32, (half, 1), 0)

    def score(cc, rc):
        columns = caps[cc].reshape(half, width)
        videos = vids[rc].reshape(tile_rows, width)
        values = logit * lax.dot_general(columns, videos, (((1,), (1,)), ((), ())), preferred_element_type=f32)
        wanted = jnp.concatenate(
            [perm_v[:, pl.ds(pl.multiple_of(dp_index(z, n, rc) * rows, rows), rows)] for n in range(inner)], axis=1
        )
        return values, (dp_index(index // ccol, i, cc) * tensor + t) * ccol + index % ccol == wanted

    tiles = [score(c, c)]
    if pair > 1:
        wait(caps.at[1 - c], fwd_rs.at[0])
        tiles.append(score(1 - c, c))
    top = functools.reduce(jnp.maximum, [jnp.max(v, axis=0, keepdims=True) for v, _ in tiles])
    expo = [jnp.exp(tile[0] - top) for tile in tiles]
    total = functools.reduce(jnp.add, [jnp.sum(v, axis=0, keepdims=True) for v in expo])
    positive = functools.reduce(jnp.add, [jnp.sum(jnp.where(h, v, 0.0), axis=0, keepdims=True) for v, h in tiles])
    stats[...] = jnp.concatenate([top, total, positive], axis=1)
    for n, k in row_offsets[::-1]:
        send(stats, stats_recv.at[n * tensor + k - 1], stats_rs.at[0], peer[n, k][1])
    for n, k in other_offsets:
        send(stats, stats_recv.at[nb - 1 + n * tensor + k], stats_rs.at[0], other_peer(n, k))
    if pair > 1:
        wait(vids.at[1 - c], cross_rs.at[0])
        cross, cross_hit = score(c, 1 - c)
    if pair * nb > 1:
        wait(stats_recv, stats_rs.at[0])

    def combine(every):
        tops = [v[:, :tile_rows] for v in every]
        row_max = functools.reduce(jnp.maximum, tops)
        sums = [v[:, tile_rows : 2 * tile_rows] * jnp.exp(m - row_max) for v, m in zip(every, tops)]
        return row_max, functools.reduce(jnp.add, sums)

    every = [stats[...]] + [stats_recv[n] for n in range(nb - 1)]
    row_max, row_sum = combine(every)
    row_pos = functools.reduce(jnp.add, [v[:, 2 * tile_rows :] for v in every])
    scale = jnp.exp(top - row_max) / row_sum
    weights = [(v * scale - tile[1].astype(f32)).astype(bf16) for v, tile in zip(expo, tiles)]

    def vid_rows(pi):
        cols = pl.ds(pl.multiple_of(pi * rows, rows), rows)
        terms = [
            lax.dot_general(
                weights_v[n, :, cols], caps[cc].reshape(half, width), (((0,), (0,)), ((), ())), preferred_element_type=f32
            )
            for n, cc in enumerate((c, 1 - c)[:pair])
        ]
        return functools.reduce(jnp.add, terms)

    for n, v in enumerate(weights):
        weights_v[n] = v
    first = rows - row_rest
    rest = pl.ds(first, row_rest)
    for n in range(1, inner):
        pi, dev = peer[n, 0]
        row_send[pi] = vid_rows(pi).astype(bf16)
        for q, (at, size) in enumerate(back):
            piece = pl.ds(at, size)
            send(row_send.at[pi, piece], row_recv.at[n - 1, piece], row_rs.at[n - 1, q], dev)
    if row_rest and pair > 1:

        @on_core(1)
        def _():
            for n in range(1, inner):
                pi, dev = peer[n, 0]
                send_on(1, row_send.at[pi, rest], row_recv.at[n - 1, rest], row_rs.at[n - 1, len(back)], dev)
    own = jnp.dot(weights[0], vids[c].reshape(tile_rows, width), preferred_element_type=f32)
    if pair > 1:
        cross_max, cross_sum = combine([stats_recv[nb - 1 + n] for n in range(nb)])
        cross = (jnp.exp(cross - cross_max) / cross_sum - cross_hit.astype(f32)).astype(bf16)
        own = own + jnp.dot(cross, vids[1 - c].reshape(tile_rows, width), preferred_element_type=f32)
    cap_acc[...] = own.reshape(outer, ccol, width)
    for k in far_first:
        pz, dev = col_peer(k)
        cap_send[k - 1] = cap_acc[pz].astype(bf16)
        send(cap_send.at[k - 1], cap_recv.at[k - 1], cg_rs.at[0], dev)
    own_rows = vid_rows(i)
    row_part[...] = own_rows
    if row_rest:
        row_send[i, rest] = own_rows[first:].astype(bf16)

        @on_core(0)
        def _():
            for n, k in row_offsets:
                pi, dev = peer[n, k]
                send_on(0, row_send.at[pi, rest], row_dir.at[n * tensor + k - 1], row_dir_rs.at[0], dev)
    loss_v[...] = row_max + jnp.log(row_sum) - row_pos
    loss_ref[...] = loss_v[:, pl.ds(pl.multiple_of(i * rows, rows), rows)]

    def clip_rows(piece, vid_grad, inverse):
        vid_grad = logit * vid_grad
        unit = unit_vid[piece]
        vid_dot = jnp.sum(unit * vid_grad, axis=1, keepdims=True)
        raw_grad = ((vid_grad - unit * vid_dot) * inverse).astype(bf16)
        clip_grad_ref[piece] = jnp.dot(raw_grad, proj_t[...], preferred_element_type=f32)

    for q, (at, size) in enumerate(back):
        piece = pl.ds(at, size)
        piece_sum = row_part[piece]
        for n in range(1, inner):
            wait(row_recv.at[n - 1, piece], row_rs.at[n - 1, q])
            piece_sum = piece_sum + row_recv[n - 1, piece].astype(f32)
        row_part[piece] = piece_sum
        sum_send[piece] = piece_sum.astype(bf16)
        for k in range(1, tensor):
            send(sum_send.at[piece], sum_recv.at[k - 1, piece], sum_rs.at[q], peer[0, k][1])
    if row_rest and pair > 1:

        @on_core(1)
        def _():
            piece_sum = row_part[rest]
            for n in range(1, inner):
                wait(row_recv.at[n - 1, rest], row_rs.at[n - 1, len(back)])
                piece_sum = piece_sum + row_recv[n - 1, rest].astype(f32)
            row_part[rest] = piece_sum
            sum_send[rest] = piece_sum.astype(bf16)
            for k in range(1, tensor):
                send_on(1, sum_send.at[rest], sum_recv.at[k - 1, rest], sum_rs.at[len(back)], peer[0, k][1])
    for q, (at, size) in enumerate(back):
        if q == min(1, len(back) - 1) and row_rest:

            @on_core(0)
            def _():
                wait(row_dir, row_dir_rs.at[0])
                terms = [row_part[rest]] + [row_dir[n].astype(f32) for n in range(nb - 1)]
                clip_rows(rest, functools.reduce(jnp.add, terms), inv_v[rest])
        piece = pl.ds(at, size)
        vid_grad = row_part[piece]
        if tensor > 1:
            wait(sum_recv.at[:, piece], sum_rs.at[q])
        for k in range(1, tensor):
            vid_grad = vid_grad + sum_recv[k - 1, piece].astype(f32)
        clip_rows(piece, vid_grad, inv_v[piece])
    if row_rest and pair > 1:

        @on_core(1)
        def _():
            vid_grad = row_part[rest]
            if tensor > 1:
                wait(sum_recv.at[:, rest], sum_rs.at[len(back)])
            for k in range(1, tensor):
                vid_grad = vid_grad + sum_recv[k - 1, rest].astype(f32)
            clip_rows(rest, vid_grad, inv_v[rest])
    cap_grad = cap_acc[z]
    if outer > 1:
        wait(cap_recv, cg_rs.at[0])
    for k in range(1, outer):
        cap_grad = cap_grad + cap_recv[k - 1].astype(f32)
    cap_grad = logit * cap_grad
    unit = cap_unit[...]
    cap_dot = jnp.sum(unit * cap_grad, axis=1, keepdims=True)
    cap_grad_ref[...] = (cap_grad - unit * cap_dot) * cap_inv
    for ref in sent:
        wait(ref, send_sem.at[0])
    for core in range(pair):
        @on_core(core)
        def _(core=core):
            for ref in sent_by[core]:
                wait(ref, send_sem.at[0])


def store_kernel(*refs):
    count = len(refs) // 2
    sems = refs[-1]
    copies = [pltpu.make_async_copy(refs[n], refs[count + n], sems.at[n]) for n in range(count)]
    for copy in copies:
        copy.start()
    for copy in copies:
        copy.wait()


def store_results(*values):
    return pl.pallas_call(
        store_kernel,
        out_shape=tuple(jax.ShapeDtypeStruct(v.shape, v.dtype) for v in values),
        in_specs=[pl.BlockSpec(memory_space=pltpu.VMEM)] * len(values),
        out_specs=tuple(pl.BlockSpec(memory_space=pltpu.HBM) for v in values),
        scratch_shapes=[pltpu.SemaphoreType.DMA((len(values),))],
        compiler_params=pltpu.CompilerParams(vmem_limit_bytes=4 * 1024 * 1024),
        name="store_results",
    )(*values)


def body(dp, tensor, clip_feats, proj_weight, caption_emb, logit_scale, pair_perm):
    rows, feats = clip_feats.shape
    ccol, width = caption_emb.shape
    outer, inner, pair = split(dp)
    nb = inner * tensor
    tile_rows = inner * rows
    vmem = pl.BlockSpec(memory_space=pltpu.VMEM)
    hbm = pl.BlockSpec(memory_space=pltpu.HBM)
    dma = pltpu.SemaphoreType.DMA
    nr, no, nt, ni = max(nb - 1, 1), max(outer - 1, 1), max(tensor - 1, 1), max(inner - 1, 1)
    forth, part_rest = pieces_of(rows, nb, forward)
    back, row_rest = pieces_of(rows, nb, backward)
    clip_grad, caption_grad, losses = pl.pallas_call(
        functools.partial(kernel, dp, tensor),
        out_shape=(
            jax.ShapeDtypeStruct((rows, feats), f32),
            jax.ShapeDtypeStruct((ccol, width), f32),
            jax.ShapeDtypeStruct((1, rows), f32),
        ),
        in_specs=[pl.BlockSpec(memory_space=pltpu.SMEM)] + [hbm] * 4,
        out_specs=(vmem, vmem, vmem),
        scratch_shapes=[
            pltpu.VMEM((1, pair_perm.shape[0]), jnp.int32),
            pltpu.VMEM((rows, feats), bf16),
            pltpu.VMEM(proj_weight.shape, bf16),
            pltpu.VMEM(proj_weight.shape[::-1], bf16),
            pltpu.VMEM((rows, width), f32),
            pltpu.VMEM((rows, width), bf16),
            pltpu.VMEM((nt, rows, width), bf16),
            pltpu.VMEM((nr, max(part_rest, 16), width), bf16),
            pltpu.VMEM((rows, width), f32),
            pltpu.VMEM((rows, 1), f32),
            pltpu.VMEM((ccol, width), bf16),
            pltpu.VMEM((pair, outer, ccol, width), bf16),
            pltpu.VMEM((ccol, width), f32),
            pltpu.VMEM((pair, inner, rows, width), bf16),
            pltpu.VMEM((1, 3 * tile_rows), f32),
            pltpu.VMEM((max(pair * nb - 1, 1), 1, 3 * tile_rows), f32),
            pltpu.VMEM((1, tile_rows), f32),
            pltpu.VMEM((pair, outer * ccol, tile_rows), bf16),
            pltpu.VMEM((outer, ccol, width), f32),
            pltpu.VMEM((rows, width), f32),
            pltpu.VMEM((inner, rows, width), bf16),
            pltpu.VMEM((ni, rows, width), bf16),
            pltpu.VMEM((nr, max(row_rest, 16), width), bf16),
            pltpu.VMEM((rows, width), bf16),
            pltpu.VMEM((nt, rows, width), bf16),
            pltpu.VMEM((no, ccol, width), bf16),
            pltpu.VMEM((no, ccol, width), bf16),
            dma((len(depths(feats)) + 3,)),
            dma((1,)),
            dma((len(forth),)),
            dma((1,)),
            dma((no,)),
            dma((1,)),
            dma((ni,)),
            dma((1,)),
            dma((ni, len(back) + 1)),
            dma((1,)),
            dma((len(back) + 1,)),
            dma((1,)),
            dma((1,)),
        ],
        compiler_params=pltpu.CompilerParams(collective_id=0, has_side_effects=True, vmem_limit_bytes=48 * 1024 * 1024),
        name="contrastive_step",
    )(
        logit_scale,
        *[
            pltpu.with_memory_space_constraint(x, pltpu.HBM)
            for x in (pair_perm.reshape(1, -1), clip_feats, proj_weight, caption_emb)
        ]
    )
    clip_grad, caption_grad, losses = store_results(clip_grad, caption_grad, losses)
    return clip_grad, caption_grad, losses.reshape(rows)


def solution(mesh):
    return jax.shard_map(
        functools.partial(body, mesh.shape["dp"], mesh.shape["tensor"]),
        mesh=mesh,
        in_specs=(P("dp", "tensor"), P("tensor", None), P(("dp", "tensor"), None), P(), P()),
        out_specs=(P("dp", "tensor"), P(("dp", "tensor"), None), P("dp")),
        check_vma=False,
    )
```
